32 devices in a mesh: grp: 2 (over x), tm: 16 (over z, y, core).
Axes of the slice: x: 2, y: 2, z: 4, core: 2. Of those that a mesh axis runs over, the one named last changes fastest.
Arguments:
- raw_frames: bfloat16 [96, 256, 256], P(('grp', 'tm')), parts along dimension 0, may hold values from 0 to 2
- angle_index: int32 [96], P('grp'), parts along dimension 0, may hold values from 0 to 2
- phase_index: int32 [96], P('grp'), parts along dimension 0, may hold values from 0 to 2
- band_shift: int32 [6, 2], P('grp'), parts along dimension 0, may hold values from 16 to 127, as said below
Outputs:
- denoised: float32 [32, 512, 512], P('grp', 'tm'), parts along dimension 0
The draws below stay inside these ranges and needn't reach their ends.
There are 2 independent parts, one for each index of `grp`. The reference program is written for one: setup_inputs(seed, part) draws one part's arguments, and reference() takes and returns one part's arrays. A program takes and returns all parts, laid end to end along the dimension named above; each array names one. Nothing has to cross between parts.
Inputs may be any that keep to these rules, and one draw needn't show every extreme that they name: `band_shift`: offsets are in cycles across the 512-pixel grid.
All inputs are finite; a program needn't handle non-finite values.
Results may differ from the reference program's by a relative error of at most 0.0049.
Values may be sent and summed in bfloat16 or wider, within the bound.
No kernel may reach another device: no remote copies, remote signals or barrier semaphores. Data moves between devices by JAX's collectives and lax.ppermute only.
A program may use at most 64 MiB of HBM per device.

```python
import jax
import jax.numpy as jnp
from jax import lax

PIX = 256
FINE = 512
SWEEPS = 2
FRAMES = 16
RAW = 48


def draw_band_shift(key, part):
    drawn_shift = jax.random.randint(jax.random.fold_in(key, 11), (6,), 16, 128)
    top_slot = jax.random.randint(jax.random.fold_in(key, 12), (), 0, 6)
    low_slot = (top_slot + 1 + jax.random.randint(jax.random.fold_in(key, 13), (), 0, 5)) % 6
    slot_index = jnp.arange(6, dtype=jnp.int32)
    values = jnp.where(slot_index == top_slot, 127, jnp.where(slot_index == low_slot, 16, drawn_shift))
    return values.reshape(3, 2).astype(jnp.int32)


def with_ends(values, rng, least, top_value):
    dims = values.shape
    index_at = [jax.random.randint(jax.random.fold_in(rng, axis), (), 0, dims[axis]) for axis in range(len(dims))]
    values = values.at[tuple(index_at)].set(least)
    longest = dims.index(max(dims))
    index_at[longest] = (index_at[longest] + 1) % dims[longest]
    return values.at[tuple(index_at)].set(top_value)


def steps_of(key, dims, split, least, high):
    gain = 1.0
    for position, blocks in split:
        steps = jax.random.uniform(jax.random.fold_in(jax.random.fold_in(key, 6), position), (blocks,), jnp.float32, least / len(split), high / len(split))
        gain = gain * jnp.repeat(jnp.exp(steps), dims[position] // blocks).reshape((-1,) + (1,) * (len(dims) - 1 - position))
    return gain


def setup_inputs(seed: int = 0, part: int = 0) -> dict:
    key_of = jax.random.split(jax.random.key(seed), 5)
    own_keys = jax.random.split(jax.random.fold_in(key_of[4], part), 5)
    raw_frames = jnp.clip(2.0 * jax.random.uniform(own_keys[0], (RAW, PIX, PIX), jnp.float32) ** steps_of(own_keys[0], (RAW, PIX, PIX), ((0, 16),), -0.2, 0.2), 0.0, 2.0).astype(jnp.bfloat16)
    angle_index = with_ends(jax.random.randint(own_keys[1], (RAW,), 0, 3), jax.random.fold_in(own_keys[1], 1), 0, 2).astype(jnp.int32)
    phase_index = with_ends(jax.random.randint(own_keys[2], (RAW,), 0, 3), jax.random.fold_in(own_keys[2], 1), 0, 2).astype(jnp.int32)
    band_shift = draw_band_shift(jax.random.fold_in(jax.random.fold_in(key_of[4], part), 71), part)
    return dict(raw_frames=raw_frames, angle_index=angle_index, phase_index=phase_index, band_shift=band_shift)


TERM_WEIGHTS = (1.0, 1.0, 1.0, 2.0, 2.0, 2.0)
STEP_SIZE = 0.01
THRESHOLD = 2.0


def half_table(coarse):
    row_index = lax.broadcasted_iota(jnp.int32, (coarse, coarse), 0)
    col_index = lax.broadcasted_iota(jnp.int32, (coarse, coarse), 1)
    offset = row_index - col_index
    parity = 1.0 - 2.0 * (offset % 2).astype(jnp.float32)
    angle_arg = jnp.pi * (offset.astype(jnp.float32) + 0.5) / coarse
    return (parity / (coarse * jnp.tan(angle_arg))).astype(jnp.bfloat16)


def wiener_table(grid_width):
    row_index = lax.broadcasted_iota(jnp.int32, (grid_width, grid_width), 0)
    col_index = lax.broadcasted_iota(jnp.int32, (grid_width, grid_width), 1)
    distance = jnp.abs(row_index - col_index)
    distance = jnp.minimum(distance, grid_width - distance)
    taps_value = -0.01 * jnp.power(0.98, (distance - 1).astype(jnp.float32))
    return jnp.where(distance == 0, 1.0, taps_value).astype(jnp.bfloat16)


def pattern_weight(angles, phases, band_shift, grid_width):
    angle_hit = angles[:, None] == jnp.arange(3, dtype=jnp.int32)[None, :]
    shift_rows = jnp.sum(jnp.where(angle_hit, band_shift[None, :, 0], 0), axis=1)
    shift_cols = jnp.sum(jnp.where(angle_hit, band_shift[None, :, 1], 0), axis=1)
    line_pos = jnp.arange(grid_width, dtype=jnp.int32)
    row_cycle = (shift_rows[:, None] * line_pos[None, :]) % grid_width
    col_cycle = (shift_cols[:, None] * line_pos[None, :]) % grid_width
    row_turn = 2.0 * jnp.pi * row_cycle.astype(jnp.float32) / grid_width
    col_turn = 2.0 * jnp.pi * ((3 * col_cycle - phases[:, None] * grid_width).astype(jnp.float32) / (3.0 * grid_width))
    row_cos = jnp.cos(row_turn)[:, :, None]
    row_sin = jnp.sin(row_turn)[:, :, None]
    col_cos = jnp.cos(col_turn)[:, None, :]
    col_sin = jnp.sin(col_turn)[:, None, :]
    return (1.0 + 2.0 * (row_cos * col_cos - row_sin * col_sin)) / 3.0


def shift_ahead(field, axis):
    count = field.shape[axis]
    tail_zero = jnp.zeros_like(lax.slice_in_dim(field, 0, 1, axis=axis))
    return jnp.concatenate([lax.slice_in_dim(field, 1, count, axis=axis), tail_zero], axis)


def shift_behind(field, axis):
    count = field.shape[axis]
    head_zero = jnp.zeros_like(lax.slice_in_dim(field, 0, 1, axis=axis))
    return jnp.concatenate([head_zero, lax.slice_in_dim(field, 0, count - 1, axis=axis)], axis)


def second_diff(field, axis):
    return shift_ahead(field, axis) - 2.0 * field + shift_behind(field, axis)


def back_diff(field, axis):
    return field - shift_behind(field, axis)


def hessian_terms(field):
    rise_rows = shift_ahead(field, 1) - field
    time_rise = shift_ahead(field, 0) - field
    return (second_diff(field, 2), second_diff(field, 1), second_diff(field, 0),
            shift_ahead(rise_rows, 2) - rise_rows,
            shift_ahead(time_rise, 2) - time_rise,
            shift_ahead(rise_rows, 0) - rise_rows)


def adjoint_sum(carried):
    carry_xx, carry_yy, carry_tt, carry_xy, carry_xt, carry_yt = carried
    result = TERM_WEIGHTS[0] * second_diff(carry_xx, 2)
    result = result + TERM_WEIGHTS[1] * second_diff(carry_yy, 1)
    result = result + TERM_WEIGHTS[2] * second_diff(carry_tt, 0)
    result = result + TERM_WEIGHTS[3] * back_diff(back_diff(carry_xy, 2), 1)
    result = result + TERM_WEIGHTS[4] * back_diff(back_diff(carry_xt, 2), 0)
    result = result + TERM_WEIGHTS[5] * back_diff(back_diff(carry_yt, 1), 0)
    return result


def reference(raw_frames, angle_index, phase_index, band_shift):
    zero_frames = jnp.zeros((3, PIX, PIX), raw_frames.dtype)
    padded_raw = jnp.concatenate([zero_frames, raw_frames, zero_frames], axis=0)
    padded_angle = jnp.pad(angle_index, (3, 3))
    padded_phase = jnp.pad(phase_index, (3, 3))
    group_count = FRAMES + 2
    raw_groups = padded_raw.reshape(group_count, 3, PIX, PIX)
    angle_groups = padded_angle.reshape(group_count, 3)
    phase_groups = padded_phase.reshape(group_count, 3)
    half_step = half_table(PIX).astype(jnp.float32)

    def group_sum(members):
        raw_block, angles, phases = members
        odd_rows = jnp.einsum('ki,fij->fkj', half_step, raw_block.astype(jnp.float32)).astype(jnp.bfloat16)
        rows_done = jnp.stack([raw_block, odd_rows], axis=2).reshape(3, FINE, PIX)
        odd_cols = jnp.einsum('fij,kj->fik', rows_done.astype(jnp.float32), half_step)
        upsampled = jnp.stack([rows_done.astype(jnp.float32), odd_cols], axis=3).reshape(3, FINE, FINE)
        return jnp.sum(pattern_weight(angles, phases, band_shift, FINE) * upsampled, axis=0)

    groups = lax.map(group_sum, (raw_groups, angle_groups, phase_groups))
    summed = (groups[:-2] + groups[1:-1] + groups[2:]).astype(jnp.bfloat16)
    wiener_column = wiener_table(FINE)[:, 0].astype(jnp.float32)
    spectrum = jnp.real(jnp.fft.fft(wiener_column))
    filtered = jnp.real(jnp.fft.ifft(spectrum[None, :, None] * jnp.fft.fft(summed.astype(jnp.float32), axis=1), axis=1)).astype(jnp.bfloat16)
    frames = jnp.real(jnp.fft.ifft(jnp.fft.fft(filtered.astype(jnp.float32), axis=2) * spectrum[None, None, :], axis=2)).astype(jnp.bfloat16)
    guide_field = frames.astype(jnp.float32)
    estimate = guide_field
    dual_terms = tuple(jnp.zeros_like(guide_field) for _ in range(6))
    for sweep_index in range(SWEEPS):
        terms = hessian_terms(estimate)
        fresh = tuple(jnp.clip(term + dual, -THRESHOLD, THRESHOLD) for term, dual in zip(terms, dual_terms))
        carried = tuple(2.0 * new_dual - dual for new_dual, dual in zip(fresh, dual_terms))
        estimate = estimate - STEP_SIZE * ((estimate - guide_field) + adjoint_sum(carried))
        dual_terms = fresh
    return estimate
```

```python
import jax
import jax.numpy as jnp
import numpy as np
from jax import lax
from jax.experimental import pallas as pl
from jax.experimental.pallas import tpu as pltpu
from jax.sharding import PartitionSpec as P

SWEEPS = 2
STEP_SIZE = 0.01
THRESHOLD = 2.0
REACH = 2 * SWEEPS
LANES = 128
SUBLANES = 8


def half_table(coarse):
    offset = np.arange(coarse)[:, None] - np.arange(coarse)[None, :]
    parity = (1.0 - 2.0 * (offset % 2)).astype(np.float32)
    angle_arg = np.float32(np.pi) * (offset.astype(np.float32) + np.float32(0.5)) / np.float32(coarse)
    return (parity / (np.float32(coarse) * np.tan(angle_arg))).astype(jnp.bfloat16)


def wiener_table(width):
    distance = np.abs(np.arange(width)[:, None] - np.arange(width)[None, :])
    distance = np.minimum(distance, width - distance)
    taps = np.float32(-0.01) * np.power(np.float32(0.98), (distance - 1).astype(np.float32))
    return np.where(distance == 0, np.float32(1.0), taps).astype(jnp.bfloat16)


def split_order(width):
    return np.concatenate([np.arange(0, width, 2), np.arange(1, width, 2)])


def window_rows_of(block_rows):
    rows = block_rows + 2 * REACH
    major = rows // SUBLANES
    stored = np.arange(rows)
    return (stored % SUBLANES) * major + stored // SUBLANES


def row_filter(wiener, blocks, block_rows):
    fine = wiener.shape[0]
    row = np.arange(blocks)[:, None] * block_rows - REACH + window_rows_of(block_rows)[None, :]
    valid = (row >= 0) & (row < fine)
    table = wiener[np.clip(row, 0, fine - 1)][:, :, split_order(fine)]
    return np.where(valid[:, :, None], table, np.zeros((), jnp.bfloat16)).reshape(-1, fine)


def dot(a, b, dims=((1,), (0,))):
    return lax.dot_general(a, b, (dims, ((), ())), preferred_element_type=jnp.float32)


def high_low(value):
    high = value.astype(jnp.bfloat16)
    return high, (value - high.astype(jnp.float32)).astype(jnp.bfloat16)


def filter_kernel(angle_ref, phase_ref, shift_ref, raw_ref, half_ref, col_ref, row_ref, out_ref, sum_ref):
    frames, coarse, _ = raw_ref.shape
    fine = 2 * coarse
    first = lax.axis_index("tm") * frames
    half_step = half_ref[...]
    lane = lax.broadcasted_iota(jnp.int32, (SUBLANES, fine), 1)
    line = lax.broadcasted_iota(jnp.int32, (SUBLANES, fine), 0)
    place = jnp.where(lane < coarse, 2 * lane, 2 * (lane - coarse) + 1)
    for f in range(frames):
        angle = angle_ref[first + f]
        phase = phase_ref[first + f]
        shift_y = shift_ref[angle, 0]
        shift_x = shift_ref[angle, 1]
        cycle = lax.rem(jnp.where(line == 0, shift_y, shift_x) * place, fine)
        turn = (3 * cycle - jnp.where(line == 0, 0, phase * fine)).astype(jnp.float32) / (3.0 * fine)
        turn = 2.0 * jnp.pi * turn
        cos_hi, cos_lo = high_low(jnp.cos(turn))
        sin_hi, sin_lo = high_low(jnp.sin(turn))
        scaled_cos = high_low((2.0 / 3.0) * jnp.cos(turn))
        scaled_sin = high_low((-2.0 / 3.0) * jnp.sin(turn))
        third = high_low(jnp.full((1, fine), 1.0 / 3.0, jnp.float32))
        ones = jnp.ones((1, fine), jnp.bfloat16)
        left = jnp.concatenate(
            [cos_hi[0:1], cos_lo[0:1], cos_hi[0:1], sin_hi[0:1], sin_lo[0:1], sin_hi[0:1], ones, ones], axis=0
        )
        right = jnp.concatenate(
            [
                scaled_cos[0][1:2], scaled_cos[0][1:2], scaled_cos[1][1:2],
                scaled_sin[0][1:2], scaled_sin[0][1:2], scaled_sin[1][1:2],
                third[0], third[1],
            ],
            axis=0,
        )
        weight = dot(left, right, ((0,), (0,)))
        raw = raw_ref[f]
        odd_rows = dot(half_step, raw).astype(jnp.bfloat16)
        rows_done = jnp.concatenate([raw, odd_rows], axis=0)
        odd_cols = dot(rows_done, half_step, ((1,), (1,)))
        even_part = weight[:, :coarse] * rows_done.astype(jnp.float32)
        odd_part = weight[:, coarse:] * odd_cols
        if f == 0:
            sum_ref[:, :coarse] = even_part
            sum_ref[:, coarse:] = odd_part
        else:
            sum_ref[:, :coarse] += even_part
            sum_ref[:, coarse:] += odd_part
    summed = sum_ref[...].astype(jnp.bfloat16)
    filtered = dot(summed, col_ref[...], ((1,), (1,))).astype(jnp.bfloat16)
    windows = dot(row_ref[...], filtered)
    out_ref[...] = windows.reshape(out_ref.shape).astype(jnp.bfloat16)


def ahead_y(parts):
    return [jnp.concatenate([v[SUBLANES:], pltpu.roll(v[:SUBLANES], SUBLANES - 1, 0)], axis=0) for v in parts]


def behind_y(parts):
    return [jnp.concatenate([pltpu.roll(v[-SUBLANES:], 1, 0), v[:-SUBLANES]], axis=0) for v in parts]


def ahead_x(parts, last_lane):
    turned = [pltpu.roll(v, LANES - 1, 1) for v in parts]
    following = turned[1:] + [jnp.zeros_like(parts[0])]
    return [jnp.where(last_lane, n, v) for v, n in zip(turned, following)]


def behind_x(parts, edge, first_lane):
    turned = [pltpu.roll(v, 1, 1) for v in parts]
    before = [edge] + turned[:-1]
    return [jnp.where(first_lane, p, v) for v, p in zip(turned, before)]


def add(a, b):
    return [x + y for x, y in zip(a, b)]


def sub(a, b):
    return [x - y for x, y in zip(a, b)]


def scale(a, factor):
    return [x * factor for x in a]


def clip(a, bound):
    return [jnp.minimum(jnp.maximum(x, -bound), bound) for x in a]


def denoise_kernel(window_ref, out_ref, guide_ref, first_ref, xx_ref, yy_ref, xy_ref, xt_ref, yt_ref, tt_ref,
                   lines_ref):
    count, rows, fine = window_ref.shape
    block_rows = rows - 2 * REACH
    major = rows // SUBLANES
    columns = fine // LANES
    blocks = [pl.ds(c * LANES, LANES) for c in range(columns)]
    lane = lax.broadcasted_iota(jnp.int32, (rows, LANES), 1)
    first_lane = lane == 0
    last_lane = lane == LANES - 1
    stored = lax.broadcasted_iota(jnp.int32, (rows, LANES), 0)
    image_row = (
        lax.axis_index("tm") * block_rows - REACH
        + lax.rem(stored, SUBLANES) * major + lax.div(stored, SUBLANES)
    )
    valid = ((image_row >= 0) & (image_row < fine)).astype(jnp.float32)
    twice_valid = 2.0 * valid

    def load(ref, t):
        return [ref[t, :, b] for b in blocks]

    def store(ref, t, parts):
        for b, v in zip(blocks, parts):
            ref[t, :, b] = v

    zero = [jnp.zeros((rows, LANES), jnp.float32)] * columns
    store(guide_ref, count, zero)
    store(guide_ref, count + 1, zero)
    store(first_ref, count, zero)
    store(first_ref, count + 1, zero)

    def window(t):
        return [window_ref[t, :, b].astype(jnp.float32) for b in blocks]

    store(guide_ref, 0, add(window(0), window(1)))
    store(guide_ref, count - 1, add(window(count - 2), window(count - 1)))

    @pl.loop(1, count - 1)
    def _(t):
        store(guide_ref, t, add(add(window(t - 1), window(t)), window(t + 1)))

    def curve_t(ref, t):
        here, after, beyond = load(ref, t), load(ref, t + 1), load(ref, t + 2)
        return sub(add(here, beyond), scale(after, 2.0))

    def sweep(ref, finish, duals):
        def settle(term, dual_ref, t, bound):
            if duals:
                dual = load(dual_ref, t)
                fresh = clip(add(term, dual), bound)
                return sub(scale(fresh, 2.0), dual)
            fresh = clip(term, bound)
            store(dual_ref, t, fresh)
            return fresh

        def step(t, carried):
            last_xt, last_yt, last_tt, this_tt = carried
            here, after = load(ref, t), load(ref, t + 1)
            rise_t = sub(after, here)
            bound = jnp.where(t + 1 < count, THRESHOLD, 0.0)
            next_tt = settle(curve_t(ref, t), tt_ref, t + 1, bound)

            rise_x = sub(ahead_x(here, last_lane), here)
            carry_xx = settle(sub(rise_x, behind_x(rise_x, here[0], first_lane)), xx_ref, t, THRESHOLD)
            flow_x = sub(ahead_x(carry_xx, last_lane), carry_xx)

            rise_y = sub(ahead_y(here), here)
            curve_y = [v * valid for v in sub(rise_y, behind_y(rise_y))]
            carry_yy = settle(curve_y, yy_ref, t, THRESHOLD)
            flow_y = sub(ahead_y(carry_yy), carry_yy)

            rise_y = [v * twice_valid for v in rise_y]
            carry_xy = settle(sub(ahead_x(rise_y, last_lane), rise_y), xy_ref, t, 2.0 * THRESHOLD)
            flow_x = add(flow_x, sub(carry_xy, behind_y(carry_xy)))

            twice_t = scale(rise_t, 2.0)
            carry_xt = settle(sub(ahead_x(twice_t, last_lane), twice_t), xt_ref, t, 2.0 * THRESHOLD)
            flow_x = add(flow_x, sub(carry_xt, last_xt))

            bend = [v * twice_valid for v in sub(ahead_y(rise_t), rise_t)]
            carry_yt = settle(bend, yt_ref, t, 2.0 * THRESHOLD)
            flow_y = add(flow_y, sub(carry_yt, last_yt))

            total = add(
                sub(flow_x, behind_x(flow_x, carry_xx[0], first_lane)), sub(flow_y, behind_y(flow_y))
            )
            curve = sub(add(next_tt, last_tt), scale(this_tt, 2.0))
            finish(t, here, add(total, curve))
            return carry_xt, carry_yt, this_tt, next_tt

        head = sub(load(ref, 1), scale(load(ref, 0), 2.0))
        first_tt = settle(head, tt_ref, 0, THRESHOLD)
        lax.fori_loop(0, count, step, (zero, zero, zero, first_tt))

    def finish_first(t, here, total):
        update = [(v - (2.0 * STEP_SIZE) * s) * valid for v, s in zip(here, total)]
        store(first_ref, t, update)

    def finish_last(t, here, total):
        for c, (v, s, g) in enumerate(zip(here, total, load(guide_ref, t))):
            update = v - STEP_SIZE * ((v - g) + s)
            for j in range(major):
                lines_ref[c, pl.ds(j, SUBLANES, stride=major), :] = update[j * SUBLANES:(j + 1) * SUBLANES]
            out_ref[t, :, blocks[c]] = lines_ref[c, pl.ds(REACH, block_rows), :]

    sweep(guide_ref, finish_first, False)
    sweep(first_ref, finish_last, True)


def shards(raw_frames, angle_index, phase_index, band_shift):
    raw_count, coarse, _ = raw_frames.shape
    fine = 2 * coarse
    tm_count = lax.axis_size("tm")
    block_rows = fine // tm_count
    window_rows = block_rows + 2 * REACH
    wiener = wiener_table(fine)
    half_step = half_table(coarse)
    col_filter = wiener[:, split_order(fine)]
    row_windows = row_filter(wiener, tm_count, block_rows)
    scalar = pl.BlockSpec(memory_space=pltpu.SMEM)
    vector = pl.BlockSpec(memory_space=pltpu.VMEM)
    windows = pl.pallas_call(
        filter_kernel,
        out_shape=jax.ShapeDtypeStruct((tm_count, window_rows, fine), jnp.bfloat16),
        in_specs=[scalar] * 3 + [vector] * 4,
        out_specs=vector,
        scratch_shapes=[pltpu.VMEM((fine, fine), jnp.float32)],
        name="filter_group",
    )(angle_index, phase_index, band_shift, raw_frames, half_step, col_filter, row_windows)
    received = lax.all_to_all(windows, "tm", split_axis=0, concat_axis=0, tiled=True)

    def field(extra):
        return pltpu.VMEM((tm_count + extra, window_rows, fine), jnp.float32)

    return pl.pallas_call(
        denoise_kernel,
        out_shape=jax.ShapeDtypeStruct((tm_count, block_rows, fine), jnp.float32),
        in_specs=[vector],
        out_specs=vector,
        scratch_shapes=[
            field(2), field(2), field(0), field(0), field(0), field(0), field(0), field(1),
            pltpu.VMEM((fine // LANES, window_rows, LANES), jnp.float32),
        ],
        name="denoise_rows",
    )(received)


def solution(mesh):
    return jax.shard_map(
        shards,
        mesh=mesh,
        in_specs=(P(("grp", "tm"), None, None), P("grp"), P("grp"), P("grp", None)),
        out_specs=P("grp", "tm", None),
        check_vma=False,
    )
```

```python
import jax
import jax.numpy as jnp
import numpy as np
from jax import lax
from jax.experimental import pallas as pl
from jax.experimental.pallas import tpu as pltpu
from jax.sharding import PartitionSpec as P

SWEEPS = 2
STEP_SIZE = 0.01
THRESHOLD = 2.0
REACH = 2 * SWEEPS
LANES = 128
SUBLANES = 8


def half_table(coarse):
    offset = np.arange(coarse)[:, None] - np.arange(coarse)[None, :]
    parity = (1.0 - 2.0 * (offset % 2)).astype(np.float32)
    angle_arg = np.float32(np.pi) * (offset.astype(np.float32) + np.float32(0.5)) / np.float32(coarse)
    return (parity / (np.float32(coarse) * np.tan(angle_arg))).astype(jnp.bfloat16)


def wiener_table(width):
    distance = np.abs(np.arange(width)[:, None] - np.arange(width)[None, :])
    distance = np.minimum(distance, width - distance)
    taps = np.float32(-0.01) * np.power(np.float32(0.98), (distance - 1).astype(np.float32))
    return np.where(distance == 0, np.float32(1.0), taps).astype(jnp.bfloat16)


def split_order(width):
    return np.concatenate([np.arange(0, width, 2), np.arange(1, width, 2)])


def window_rows_of(block_rows):
    rows = block_rows + 2 * REACH
    major = rows // SUBLANES
    stored = np.arange(rows)
    return (stored % SUBLANES) * major + stored // SUBLANES


def columns_of(fine):
    stored = np.arange(fine)
    return (stored % LANES) * (fine // LANES) + stored // LANES


def row_filter(wiener, blocks, block_rows):
    fine = wiener.shape[0]
    row = np.arange(blocks)[:, None] * block_rows - REACH + window_rows_of(block_rows)[None, :]
    valid = (row >= 0) & (row < fine)
    table = wiener[np.clip(row, 0, fine - 1)][:, :, split_order(fine)]
    return np.where(valid[:, :, None], table, np.zeros((), jnp.bfloat16)).reshape(-1, fine)


def dot(a, b, dims=((1,), (0,))):
    return lax.dot_general(a, b, (dims, ((), ())), preferred_element_type=jnp.float32)


def high_low(value):
    high = value.astype(jnp.bfloat16)
    return high, (value - high.astype(jnp.float32)).astype(jnp.bfloat16)


def filter_kernel(angle_ref, phase_ref, shift_ref, raw_ref, half_ref, col_ref, row_ref, out_ref, sum_ref):
    frames, coarse, _ = raw_ref.shape
    fine = 2 * coarse
    first = lax.axis_index("tm") * frames
    half_step = half_ref[...]
    lane = lax.broadcasted_iota(jnp.int32, (SUBLANES, fine), 1)
    line = lax.broadcasted_iota(jnp.int32, (SUBLANES, fine), 0)
    place = jnp.where(lane < coarse, 2 * lane, 2 * (lane - coarse) + 1)
    for f in range(frames):
        angle = angle_ref[first + f]
        phase = phase_ref[first + f]
        shift_y = shift_ref[0, angle]
        shift_x = shift_ref[1, angle]
        cycle = lax.rem(jnp.where(line == 0, shift_y, shift_x) * place, fine)
        turn = (3 * cycle - jnp.where(line == 0, 0, phase * fine)).astype(jnp.float32) / (3.0 * fine)
        turn = 2.0 * jnp.pi * turn
        cos_hi, cos_lo = high_low(jnp.cos(turn))
        sin_hi, sin_lo = high_low(jnp.sin(turn))
        scaled_cos = high_low((2.0 / 3.0) * jnp.cos(turn))
        scaled_sin = high_low((-2.0 / 3.0) * jnp.sin(turn))
        third = high_low(jnp.full((1, fine), 1.0 / 3.0, jnp.float32))
        ones = jnp.ones((1, fine), jnp.bfloat16)
        left = jnp.concatenate(
            [cos_hi[0:1], cos_lo[0:1], cos_hi[0:1], sin_hi[0:1], sin_lo[0:1], sin_hi[0:1], ones, ones], axis=0
        )
        right = jnp.concatenate(
            [
                scaled_cos[0][1:2], scaled_cos[0][1:2], scaled_cos[1][1:2],
                scaled_sin[0][1:2], scaled_sin[0][1:2], scaled_sin[1][1:2],
                third[0], third[1],
            ],
            axis=0,
        )
        weight = dot(left, right, ((0,), (0,)))
        raw = raw_ref[f]
        odd_rows = dot(half_step, raw).astype(jnp.bfloat16)
        rows_done = jnp.concatenate([raw, odd_rows], axis=0)
        odd_cols = dot(rows_done, half_step, ((1,), (1,)))
        even_part = weight[:, :coarse] * rows_done.astype(jnp.float32)
        odd_part = weight[:, coarse:] * odd_cols
        if f == 0:
            sum_ref[:, :coarse] = even_part
            sum_ref[:, coarse:] = odd_part
        else:
            sum_ref[:, :coarse] += even_part
            sum_ref[:, coarse:] += odd_part
    summed = sum_ref[...].astype(jnp.bfloat16)
    filtered = dot(summed, col_ref[...], ((1,), (1,))).astype(jnp.bfloat16)
    windows = dot(row_ref[...], filtered)
    out_ref[...] = windows.reshape(out_ref.shape).astype(jnp.bfloat16)


def add(a, b):
    return [[x + y for x, y in zip(p, q)] for p, q in zip(a, b)]


def sub(a, b):
    return [[x - y for x, y in zip(p, q)] for p, q in zip(a, b)]


def times(a, factor):
    return [[x * factor for x in p] for p in a]


def by_row(a, factors):
    return [[x * f for x in p] for p, f in zip(a, factors)]


def clip(a, bound):
    return [[jnp.minimum(jnp.maximum(x, -bound), bound) for x in p] for p in a]


def ahead_y(a):
    return a[1:] + [[pltpu.roll(x, SUBLANES - 1, 0) for x in a[0]]]


def behind_y(a):
    return [[pltpu.roll(x, 1, 0) for x in a[-1]]] + a[:-1]


def ahead_x(a, last_lane):
    return [
        p[1:] + [jnp.where(last_lane, 0.0, pltpu.roll(p[0], LANES - 1, 1))] for p in a
    ]


def behind_x(a, first_lane, edge=None):
    return [
        [jnp.where(first_lane, 0.0 if edge is None else edge[j][0], pltpu.roll(p[-1], 1, 1))] + p[:-1]
        for j, p in enumerate(a)
    ]


def denoise_kernel(window_ref, order_ref, out_ref, guide_ref, first_ref, xx_ref, yy_ref, xy_ref, xt_ref, yt_ref, tt_ref,
                   past_ref, curve_ref, lines_ref, turned_ref):
    count, rows, fine = window_ref.shape
    block_rows = rows - 2 * REACH
    major = rows // SUBLANES
    columns = fine // LANES
    tiles = [
        [(pl.ds(j * SUBLANES, SUBLANES), pl.ds(c * LANES, LANES)) for c in range(columns)] for j in range(major)
    ]
    lane = lax.broadcasted_iota(jnp.int32, (SUBLANES, LANES), 1)
    first_lane = lane == 0
    last_lane = lane == LANES - 1
    sublane = lax.broadcasted_iota(jnp.int32, (SUBLANES, LANES), 0)
    top_row = lax.axis_index("tm") * block_rows - REACH
    valid, twice_valid, twice_step = [], [], []
    for j in range(major):
        image_row = top_row + sublane * major + j
        inside = (image_row >= 0) & (image_row < fine)
        valid.append(jnp.where(inside, 1.0, 0.0))
        twice_valid.append(jnp.where(inside, 2.0, 0.0))
        twice_step.append(jnp.where(inside, 2.0 * STEP_SIZE, 0.0))

    def load(ref, t):
        return [[ref[(t, *tile)] for tile in line] for line in tiles]

    def store(ref, t, values):
        for line, p in zip(tiles, values):
            for tile, x in zip(line, p):
                ref[(t, *tile)] = x

    zero = [[jnp.zeros((SUBLANES, LANES), jnp.float32)] * columns] * major

    def window(t):
        parts = [window_ref[t, :, pl.ds(c * LANES, LANES)].astype(jnp.float32) for c in range(columns)]
        return [[v[j * SUBLANES:(j + 1) * SUBLANES] for v in parts] for j in range(major)]

    def close(ref):
        store(ref, count, zero)
        store(ref, count + 1, times(load(ref, count - 1), -1.0))

    store(guide_ref, 0, add(window(0), window(1)))
    store(guide_ref, count - 1, add(window(count - 2), window(count - 1)))
    close(guide_ref)

    def gather(t, carried):
        store(guide_ref, t, add(add(window(t - 1), window(t)), window(t + 1)))
        return carried

    lax.fori_loop(1, count - 1, gather, 0)

    def sweep(ref, finish, duals, before_pair=None):
        def settle(term, dual_ref, t, bound):
            if duals:
                return clip(add(term, load(dual_ref, t)), bound)
            fresh = clip(term, bound)
            store(dual_ref, t, fresh)
            return fresh

        def frame(t):
            here = load(ref, t)
            rise_x = sub(ahead_x(here, last_lane), here)
            fresh_xx = settle(sub(rise_x, behind_x(rise_x, first_lane, here)), xx_ref, t, THRESHOLD)
            flow_x = sub(ahead_x(fresh_xx, last_lane), fresh_xx)
            rise_y = sub(ahead_y(here), here)
            double_rise = by_row(rise_y, twice_valid)
            fresh_xy = settle(sub(ahead_x(double_rise, last_lane), double_rise), xy_ref, t, 2.0 * THRESHOLD)
            flow_x = add(flow_x, sub(fresh_xy, behind_y(fresh_xy)))
            total = sub(flow_x, behind_x(flow_x, first_lane, fresh_xx))

            curve_y = by_row(sub(rise_y, behind_y(rise_y)), valid)
            fresh_yy = settle(curve_y, yy_ref, t, THRESHOLD)
            flow_y = sub(ahead_y(fresh_yy), fresh_yy)
            total = add(total, sub(flow_y, behind_y(flow_y)))

            after = load(ref, t + 1)
            rise_t = sub(after, here)
            twice_t = times(rise_t, 2.0)
            fresh_xt = settle(sub(ahead_x(twice_t, last_lane), twice_t), xt_ref, t, 2.0 * THRESHOLD)
            bend = by_row(sub(ahead_y(rise_t), rise_t), twice_valid)
            fresh_yt = settle(bend, yt_ref, t, 2.0 * THRESHOLD)
            flow_t = add(sub(fresh_xt, behind_x(fresh_xt, first_lane)), sub(fresh_yt, behind_y(fresh_yt)))
            next_tt = settle(sub(sub(load(ref, t + 2), after), rise_t), tt_ref, t + 1, THRESHOLD)
            flow_t = add(flow_t, sub(next_tt, load(curve_ref, 0)))
            total = add(total, sub(flow_t, load(past_ref, 0)))
            store(past_ref, 0, flow_t)
            store(curve_ref, 0, next_tt)
            finish(t, here, total)

        def pair(k, carried):
            if before_pair is not None:
                before_pair(jnp.maximum(k - 1, 0))
            frame(2 * k)
            frame(2 * k + 1)
            return carried

        start = load(ref, 0)
        first_tt = settle(sub(sub(load(ref, 1), start), start), tt_ref, 0, THRESHOLD)
        store(curve_ref, 0, first_tt)
        store(past_ref, 0, first_tt)
        lax.fori_loop(0, count // 2, pair, 0)

    def finish_first(t, here, total):
        store(first_ref, t, sub(here, by_row(total, twice_step)))

    def finish_last(t, here, total):
        change = sub(load(guide_ref, t), here)
        update = sub(add(here, times(change, STEP_SIZE + 0.5)), times(total, 2.0 * STEP_SIZE))
        slot = lax.rem(t, 2) * block_rows
        for c in range(columns):
            for j in range(major):
                lines_ref[c, pl.ds(j, SUBLANES, stride=major), :] = update[j][c]
            high, low = high_low(lines_ref[c, pl.ds(REACH, block_rows), :])
            turned_ref[pl.ds(slot, block_rows), pl.ds(c * LANES, LANES)] = high
            turned_ref[pl.ds(2 * block_rows + slot, block_rows), pl.ds(c * LANES, LANES)] = low

    def reorder(k):
        both = dot(turned_ref[...], order_ref[...])
        both = both[:2 * block_rows] + both[2 * block_rows:]
        out_ref[pl.ds(2 * k, 2)] = both.reshape(2, block_rows, fine)

    sweep(guide_ref, finish_first, False)
    close(first_ref)
    turned_ref[...] = jnp.zeros_like(turned_ref)
    sweep(first_ref, finish_last, True, reorder)
    reorder(count // 2 - 1)


def shards(raw_frames, angle_index, phase_index, band_shift):
    raw_count, coarse, _ = raw_frames.shape
    fine = 2 * coarse
    tm_count = lax.axis_size("tm")
    block_rows = fine // tm_count
    window_rows = block_rows + 2 * REACH
    wiener = wiener_table(fine)
    half_step = half_table(coarse)
    col_filter = wiener[columns_of(fine)][:, split_order(fine)]
    row_windows = row_filter(wiener, tm_count, block_rows)
    order = np.eye(fine, dtype=jnp.bfloat16)[columns_of(fine)]
    scalar = pl.BlockSpec(memory_space=pltpu.SMEM)
    vector = pl.BlockSpec(memory_space=pltpu.VMEM)
    windows = pl.pallas_call(
        filter_kernel,
        out_shape=jax.ShapeDtypeStruct((tm_count, window_rows, fine), jnp.bfloat16),
        in_specs=[scalar] * 3 + [vector] * 4,
        out_specs=vector,
        scratch_shapes=[pltpu.VMEM((fine, fine), jnp.float32)],
        name="filter_group",
    )(angle_index, phase_index, band_shift.T, raw_frames, half_step, col_filter, row_windows)
    received = lax.all_to_all(windows, "tm", split_axis=0, concat_axis=0, tiled=True)

    def field(frames):
        return pltpu.VMEM((frames, window_rows, fine), jnp.float32)

    return pl.pallas_call(
        denoise_kernel,
        out_shape=jax.ShapeDtypeStruct((tm_count, block_rows, fine), jnp.float32),
        in_specs=[vector] * 2,
        out_specs=vector,
        scratch_shapes=[
            field(tm_count + 2), field(tm_count + 2), *[field(tm_count)] * 5, field(tm_count + 1),
            field(1), field(1), pltpu.VMEM((fine // LANES, window_rows, LANES), jnp.float32),
            pltpu.VMEM((4 * block_rows, fine), jnp.bfloat16),
        ],
        name="denoise_rows",
    )(received, order)


def solution(mesh):
    return jax.shard_map(
        shards,
        mesh=mesh,
        in_specs=(P(("grp", "tm"), None, None), P("grp"), P("grp"), P("grp", None)),
        out_specs=P("grp", "tm", None),
        check_vma=False,
    )
```

```python
import jax
import jax.numpy as jnp
import numpy as np
from jax import lax
from jax.experimental import pallas as pl
from jax.experimental.pallas import tpu as pltpu
from jax.sharding import PartitionSpec as P

SWEEPS = 2
STEP_SIZE = 0.01
THRESHOLD = 2.0
REACH = 2 * SWEEPS
LANES = 128
SUBLANES = 8


def half_table(coarse):
    offset = np.arange(coarse)[:, None] - np.arange(coarse)[None, :]
    parity = (1.0 - 2.0 * (offset % 2)).astype(np.float32)
    angle_arg = np.float32(np.pi) * (offset.astype(np.float32) + np.float32(0.5)) / np.float32(coarse)
    return (parity / (np.float32(coarse) * np.tan(angle_arg))).astype(jnp.bfloat16)


def wiener_table(width):
    distance = np.abs(np.arange(width)[:, None] - np.arange(width)[None, :])
    distance = np.minimum(distance, width - distance)
    taps = np.float32(-0.01) * np.power(np.float32(0.98), (distance - 1).astype(np.float32))
    return np.where(distance == 0, np.float32(1.0), taps).astype(jnp.bfloat16)


def split_order(width):
    return np.concatenate([np.arange(0, width, 2), np.arange(1, width, 2)])


def columns_of(fine):
    stored = np.arange(fine)
    return (stored % LANES) * (fine // LANES) + stored // LANES


def row_filter(wiener, blocks, block_rows):
    fine = wiener.shape[0]
    row = np.arange(blocks)[:, None] * block_rows + np.arange(-REACH, block_rows + REACH)[None, :]
    valid = (row >= 0) & (row < fine)
    table = wiener[np.clip(row, 0, fine - 1)][:, :, split_order(fine)]
    return np.where(valid[:, :, None], table, np.zeros((), jnp.bfloat16)).reshape(-1, fine)


def exchange_order(chips):
    bits = chips.bit_length() - 1
    flipped = [int(format(k, "b").zfill(bits)[::-1], 2) for k in range(1, chips)]
    return [k for k in flipped if k != 1] + [1]


def dot(a, b, dims=((1,), (0,))):
    return lax.dot_general(a, b, (dims, ((), ())), preferred_element_type=jnp.float32)


def high_low(value):
    high = value.astype(jnp.bfloat16)
    return high, (value - high.astype(jnp.float32)).astype(jnp.bfloat16)


def pattern_factors(angle, phase, shift_ref, fine):
    lane = lax.broadcasted_iota(jnp.int32, (SUBLANES, fine), 1)
    line = lax.broadcasted_iota(jnp.int32, (SUBLANES, fine), 0)
    place = jnp.where(lane < fine // 2, 2 * lane, 2 * lane - fine + 1)
    cycle = lax.rem(jnp.where(line == 0, shift_ref[0, angle], shift_ref[1, angle]) * place, fine)
    turn = (3 * cycle - jnp.where(line == 0, 0, phase * fine)).astype(jnp.float32) / (3.0 * fine)
    turn = 2.0 * jnp.pi * turn
    cosine, sine = jnp.cos(turn), jnp.sin(turn)
    row_cos, row_sin = high_low(cosine[0:1]), high_low(sine[0:1])
    col_cos, col_sin = high_low((2.0 / 3.0) * cosine[1:2]), high_low((-2.0 / 3.0) * sine[1:2])
    third = high_low(jnp.full((1, fine), 1.0 / 3.0, jnp.float32))
    ones = jnp.ones((1, fine), jnp.bfloat16)
    left = [row_cos[0], row_cos[1], row_cos[0], row_sin[0], row_sin[1], row_sin[0], ones, ones]
    right = [col_cos[0], col_cos[0], col_cos[1], col_sin[0], col_sin[0], col_sin[1], third[0], third[1]]
    return jnp.concatenate(left, axis=0), jnp.concatenate(right, axis=0)


def filter_kernel(angle_hbm, phase_hbm, shift_hbm, raw_hbm, half_hbm, col_hbm, row_hbm, *refs):
    *out_refs, angle_ref, phase_ref, shift_ref, raw_ref, half_ref, col_ref, row_ref = refs[:-4]
    rows_ref, sum_ref, window_ref, arrived = refs[-4:]
    sources = (angle_hbm, phase_hbm, shift_hbm, raw_hbm, half_hbm, col_hbm, row_hbm)
    targets = (angle_ref, phase_ref, shift_ref, raw_ref, half_ref, col_ref, row_ref)
    copies = [
        pltpu.make_async_copy(source, target, arrived.at[i])
        for i, (source, target) in enumerate(zip(sources, targets))
    ]
    for copy in copies:
        copy.start()
    frames, coarse, _ = raw_ref.shape
    fine = 2 * coarse
    first = lax.axis_index("tm") * frames
    chip = lax.axis_index("tm") // 2
    for copy in copies[:3]:
        copy.wait()
    factors = [
        pattern_factors(angle_ref[first + f], phase_ref[first + f], shift_ref, fine) for f in range(frames)
    ]
    copies[3].wait()
    copies[4].wait()
    half_step = half_ref[...]
    for f in range(frames):
        rows_ref[f, :coarse] = raw_ref[f]
        rows_ref[f, coarse:] = dot(half_step, raw_ref[f]).astype(jnp.bfloat16)
    for r in range(0, fine, 2 * LANES):
        even, odd = 0.0, 0.0
        for f, (left, right) in enumerate(factors):
            rows_done = rows_ref[f, r:r + 2 * LANES]
            weight = dot(left[:, r:r + 2 * LANES], right, ((0,), (0,)))
            even += weight[:, :coarse] * rows_done.astype(jnp.float32)
            odd += weight[:, coarse:] * dot(rows_done, half_step, ((1,), (1,)))
        sum_ref[r:r + 2 * LANES, :coarse] = even.astype(jnp.bfloat16)
        sum_ref[r:r + 2 * LANES, coarse:] = odd.astype(jnp.bfloat16)
    copies[5].wait()
    filtered = dot(sum_ref[...], col_ref[...], ((1,), (1,))).astype(jnp.bfloat16)
    copies[6].wait()
    window_ref[...] = dot(row_ref[...], filtered).reshape(window_ref.shape).astype(jnp.bfloat16)
    for k, out_ref in enumerate(out_refs):
        out_ref[...] = window_ref[chip ^ k]


def on_core(core, rows, body):
    for c in range(2):
        @pl.when(core == c)
        def _(c=c):
            body(c * rows)


def partner_kernel(*refs):
    *in_refs, out_ref = refs
    rows = out_ref.shape[1]

    def take(start):
        for k, in_ref in enumerate(in_refs):
            out_ref[k] = in_ref[start:start + rows]

    on_core(1 - lax.axis_index("tm") % 2, rows - 2 * REACH, take)


def add(a, b):
    return [[x + y for x, y in zip(p, q)] for p, q in zip(a, b)]


def sub(a, b):
    return [[x - y for x, y in zip(p, q)] for p, q in zip(a, b)]


def times(a, factor):
    return [[x * factor for x in p] for p in a]


def by_row(a, factors):
    return [[x * f for x in p] for p, f in zip(a, factors)]


def clip(a, bound):
    return [[jnp.minimum(jnp.maximum(x, -bound), bound) for x in p] for p in a]


def ahead_y(a):
    return a[1:] + [[pltpu.roll(x, SUBLANES - 1, 0) for x in a[0]]]


def behind_y(a):
    return [[pltpu.roll(x, 1, 0) for x in a[-1]]] + a[:-1]


def ahead_x(a, last_lane):
    return [
        p[1:] + [jnp.where(last_lane, 0.0, pltpu.roll(p[0], LANES - 1, 1))] for p in a
    ]


def behind_x(a, first_lane, edge=None):
    return [
        [jnp.where(first_lane, 0.0 if edge is None else edge[j][0], pltpu.roll(p[-1], 1, 1))] + p[:-1]
        for j, p in enumerate(a)
    ]


def denoise_kernel(*refs):
    *own_refs, partner_ref, order_ref, out_ref, window_ref = refs[:-12]
    denoise(window_ref, order_ref, out_ref, *refs[-12:], own_refs=own_refs, partner_ref=partner_ref)


def denoise(window_ref, order_ref, out_ref, guide_ref, first_ref, xx_ref, yy_ref, xy_ref, xt_ref, yt_ref, tt_ref,
                   past_ref, curve_ref, lines_ref, turned_ref, own_refs, partner_ref):
    count, rows, fine = window_ref.shape
    block_rows = rows - 2 * REACH
    major = rows // SUBLANES
    columns = fine // LANES
    tiles = [
        [(pl.ds(j * SUBLANES, SUBLANES), pl.ds(c * LANES, LANES)) for c in range(columns)] for j in range(major)
    ]
    lane = lax.broadcasted_iota(jnp.int32, (SUBLANES, LANES), 1)
    first_lane = lane == 0
    last_lane = lane == LANES - 1
    sublane = lax.broadcasted_iota(jnp.int32, (SUBLANES, LANES), 0)
    top_row = lax.axis_index("tm") * block_rows - REACH
    valid, twice_valid, twice_step = [], [], []
    for j in range(major):
        image_row = top_row + sublane * major + j
        inside = (image_row >= 0) & (image_row < fine)
        valid.append(jnp.where(inside, 1.0, 0.0))
        twice_valid.append(jnp.where(inside, 2.0, 0.0))
        twice_step.append(jnp.where(inside, 2.0 * STEP_SIZE, 0.0))

    def load(ref, t):
        return [[ref[(t, *tile)] for tile in line] for line in tiles]

    def store(ref, t, values):
        for line, p in zip(tiles, values):
            for tile, x in zip(line, p):
                ref[(t, *tile)] = x

    zero = [[jnp.zeros((SUBLANES, LANES), jnp.float32)] * columns] * major

    chip, core = lax.axis_index("tm") // 2, lax.axis_index("tm") % 2

    def place(start):
        for k, own_ref in enumerate(own_refs):
            window_ref[2 * (chip ^ k) + core] = own_ref[start:start + rows]

    on_core(core, block_rows, place)
    for k in range(count // 2):
        window_ref[2 * (chip ^ k) + 1 - core] = partner_ref[k]

    def window(t):
        return [window_ref[t, :, pl.ds(c * LANES, LANES)].astype(jnp.float32) for c in range(columns)]

    def keep_sum(t, *frames):
        for c, parts in enumerate(zip(*[window(f) for f in frames])):
            lines_ref[c] = sum(parts[1:], parts[0])
            for j in range(major):
                guide_ref[t, pl.ds(j * SUBLANES, SUBLANES), pl.ds(c * LANES, LANES)] = lines_ref[
                    c, pl.ds(j, SUBLANES, stride=major), :
                ]

    def close(ref):
        store(ref, count, zero)
        store(ref, count + 1, times(load(ref, count - 1), -1.0))

    keep_sum(0, 0, 1)
    keep_sum(count - 1, count - 2, count - 1)
    close(guide_ref)

    def gather(t, carried):
        keep_sum(t, t - 1, t, t + 1)
        return carried

    lax.fori_loop(1, count - 1, gather, 0)

    def sweep(ref, finish, duals, before_pair=None):
        def settle(term, dual_ref, t, bound):
            if duals:
                return clip(add(term, load(dual_ref, t)), bound)
            fresh = clip(term, bound)
            store(dual_ref, t, fresh)
            return fresh

        def frame(t):
            here = load(ref, t)
            rise_x = sub(ahead_x(here, last_lane), here)
            fresh_xx = settle(sub(rise_x, behind_x(rise_x, first_lane, here)), xx_ref, t, THRESHOLD)
            flow_x = sub(ahead_x(fresh_xx, last_lane), fresh_xx)
            rise_y = sub(ahead_y(here), here)
            double_rise = by_row(rise_y, twice_valid)
            fresh_xy = settle(sub(ahead_x(double_rise, last_lane), double_rise), xy_ref, t, 2.0 * THRESHOLD)
            flow_x = add(flow_x, sub(fresh_xy, behind_y(fresh_xy)))
            total = sub(flow_x, behind_x(flow_x, first_lane, fresh_xx))

            curve_y = by_row(sub(rise_y, behind_y(rise_y)), valid)
            fresh_yy = settle(curve_y, yy_ref, t, THRESHOLD)
            flow_y = sub(ahead_y(fresh_yy), fresh_yy)
            total = add(total, sub(flow_y, behind_y(flow_y)))

            after = load(ref, t + 1)
            rise_t = sub(after, here)
            twice_t = times(rise_t, 2.0)
            fresh_xt = settle(sub(ahead_x(twice_t, last_lane), twice_t), xt_ref, t, 2.0 * THRESHOLD)
            bend = by_row(sub(ahead_y(rise_t), rise_t), twice_valid)
            fresh_yt = settle(bend, yt_ref, t, 2.0 * THRESHOLD)
            flow_t = add(sub(fresh_xt, behind_x(fresh_xt, first_lane)), sub(fresh_yt, behind_y(fresh_yt)))
            next_tt = settle(sub(sub(load(ref, t + 2), after), rise_t), tt_ref, t + 1, THRESHOLD)
            flow_t = add(flow_t, sub(next_tt, load(curve_ref, 0)))
            total = add(total, sub(flow_t, load(past_ref, 0)))
            store(past_ref, 0, flow_t)
            store(curve_ref, 0, next_tt)
            finish(t, here, total)

        def pair(k, carried):
            if before_pair is not None:
                before_pair(jnp.maximum(k - 1, 0))
            frame(2 * k)
            frame(2 * k + 1)
            return carried

        start = load(ref, 0)
        first_tt = settle(sub(sub(load(ref, 1), start), start), tt_ref, 0, THRESHOLD)
        store(curve_ref, 0, first_tt)
        store(past_ref, 0, first_tt)
        lax.fori_loop(0, count // 2, pair, 0)

    def finish_first(t, here, total):
        store(first_ref, t, sub(here, by_row(total, twice_step)))

    def finish_last(t, here, total):
        change = sub(load(guide_ref, t), here)
        update = sub(add(here, times(change, STEP_SIZE + 0.5)), times(total, 2.0 * STEP_SIZE))
        slot = lax.rem(t, 2) * block_rows
        for c in range(columns):
            for j in range(major):
                lines_ref[c, pl.ds(j, SUBLANES, stride=major), :] = update[j][c]
            high, low = high_low(lines_ref[c, pl.ds(REACH, block_rows), :])
            turned_ref[pl.ds(slot, block_rows), pl.ds(c * LANES, LANES)] = high
            turned_ref[pl.ds(2 * block_rows + slot, block_rows), pl.ds(c * LANES, LANES)] = low

    def reorder(k):
        both = dot(turned_ref[...], order_ref[...])
        both = both[:2 * block_rows] + both[2 * block_rows:]
        out_ref[pl.ds(2 * k, 2)] = both.reshape(2, block_rows, fine)

    sweep(guide_ref, finish_first, False)
    close(first_ref)
    turned_ref[...] = jnp.zeros_like(turned_ref)
    sweep(first_ref, finish_last, True, reorder)
    reorder(count // 2 - 1)


def shards(raw_frames, angle_index, phase_index, band_shift):
    raw_count, coarse, _ = raw_frames.shape
    fine = 2 * coarse
    tm_count = lax.axis_size("tm")
    chips = tm_count // 2
    block_rows = fine // tm_count
    window_rows = block_rows + 2 * REACH
    chip_rows = 2 * block_rows + 2 * REACH
    wiener = wiener_table(fine)
    half_step = half_table(coarse)
    col_filter = wiener[columns_of(fine)][:, split_order(fine)]
    row_windows = row_filter(wiener, chips, 2 * block_rows)
    order = np.eye(fine, dtype=jnp.bfloat16)[columns_of(fine)]
    sources = (angle_index, phase_index, band_shift.T, raw_frames, half_step, col_filter, row_windows)
    vector = pl.BlockSpec(memory_space=pltpu.VMEM)
    frames = pl.pallas_call(
        filter_kernel,
        out_shape=[jax.ShapeDtypeStruct((chip_rows, fine), jnp.bfloat16)] * chips,
        in_specs=[pl.BlockSpec(memory_space=pltpu.HBM)] * len(sources),
        out_specs=[vector] * chips,
        scratch_shapes=[
            *[pltpu.SMEM(v.shape, v.dtype) for v in sources[:3]],
            *[pltpu.VMEM(v.shape, v.dtype) for v in sources[3:]],
            pltpu.VMEM((raw_count, fine, coarse), jnp.bfloat16), pltpu.VMEM((fine, fine), jnp.bfloat16),
            pltpu.VMEM((chips, chip_rows, fine), jnp.bfloat16), pltpu.SemaphoreType.DMA((len(sources),)),
        ],
        name="filter_group",
    )(*sources)
    received = list(frames)
    for k in reversed(exchange_order(chips)):
        received[k] = lax.ppermute(frames[k], "tm", [(i, i ^ (2 * k)) for i in range(tm_count)])
    windows = jax.ShapeDtypeStruct((chips, window_rows, fine), jnp.bfloat16)
    partner = pl.pallas_call(
        partner_kernel,
        out_shape=windows,
        in_specs=[vector] * chips,
        out_specs=vector,
        compiler_params=pltpu.CompilerParams(vmem_limit_bytes=8 << 20),
        name="partner_rows",
    )(*received)
    partner = lax.ppermute(partner, "tm", [(i, i ^ 1) for i in range(tm_count)])

    def field(frames):
        return pltpu.VMEM((frames, window_rows, fine), jnp.float32)

    return pl.pallas_call(
        denoise_kernel,
        out_shape=jax.ShapeDtypeStruct((tm_count, block_rows, fine), jnp.float32),
        in_specs=[vector] * (chips + 2),
        out_specs=vector,
        scratch_shapes=[
            pltpu.VMEM((tm_count, window_rows, fine), jnp.bfloat16),
            field(tm_count + 2), field(tm_count + 2), *[field(tm_count)] * 5, field(tm_count + 1),
            field(1), field(1), pltpu.VMEM((fine // LANES, window_rows, LANES), jnp.float32),
            pltpu.VMEM((4 * block_rows, fine), jnp.bfloat16),
        ],
        compiler_params=pltpu.CompilerParams(vmem_limit_bytes=40 << 20),
        name="denoise_rows",
    )(*received, partner, order)


def solution(mesh):
    return jax.shard_map(
        shards,
        mesh=mesh,
        in_specs=(P(("grp", "tm"), None, None), P("grp"), P("grp"), P("grp", None)),
        out_specs=P("grp", "tm", None),
        check_vma=False,
    )
```

```python
from functools import partial

import jax
import jax.numpy as jnp
import numpy as np
from jax import lax
from jax.experimental import pallas as pl
from jax.experimental.pallas import tpu as pltpu
from jax.sharding import PartitionSpec as P

SWEEPS = 2
STEP_SIZE = 0.01
THRESHOLD = 2.0
REACH = 2 * SWEEPS
LANES = 128
SUBLANES = 8


def half_table(coarse):
    offset = np.arange(coarse)[:, None] - np.arange(coarse)[None, :]
    parity = (1.0 - 2.0 * (offset % 2)).astype(np.float32)
    angle_arg = np.float32(np.pi) * (offset.astype(np.float32) + np.float32(0.5)) / np.float32(coarse)
    return (parity / (np.float32(coarse) * np.tan(angle_arg))).astype(jnp.bfloat16)


def wiener_table(width):
    distance = np.abs(np.arange(width)[:, None] - np.arange(width)[None, :])
    distance = np.minimum(distance, width - distance)
    taps = np.float32(-0.01) * np.power(np.float32(0.98), (distance - 1).astype(np.float32))
    return np.where(distance == 0, np.float32(1.0), taps).astype(jnp.bfloat16)


def split_order(width):
    return np.concatenate([np.arange(0, width, 2), np.arange(1, width, 2)])


def columns_of(fine):
    stored = np.arange(fine)
    return (stored % LANES) * (fine // LANES) + stored // LANES


def row_filter(wiener, blocks, block_rows):
    fine = wiener.shape[0]
    row = np.arange(blocks)[:, None] * block_rows + np.arange(-REACH, block_rows + REACH)[None, :]
    valid = (row >= 0) & (row < fine)
    table = wiener[np.clip(row, 0, fine - 1)][:, :, split_order(fine)]
    return np.where(valid[:, :, None], table, np.zeros((), jnp.bfloat16)).reshape(-1, fine)


def exchange_order(chips):
    bits = chips.bit_length() - 1
    flipped = [int(format(k, "b").zfill(bits)[::-1], 2) for k in range(1, chips)]
    return [k for k in flipped if k != 1] + [1]


def dot(a, b, dims=((1,), (0,))):
    return lax.dot_general(a, b, (dims, ((), ())), preferred_element_type=jnp.float32)


def high_low(value):
    high = value.astype(jnp.bfloat16)
    return high, (value - high.astype(jnp.float32)).astype(jnp.bfloat16)


def pattern_factors(angle, phase, shift_ref, fine):
    lane = lax.broadcasted_iota(jnp.int32, (SUBLANES, fine), 1)
    line = lax.broadcasted_iota(jnp.int32, (SUBLANES, fine), 0)
    place = jnp.where(lane < fine // 2, 2 * lane, 2 * lane - fine + 1)
    cycle = lax.rem(jnp.where(line == 0, shift_ref[0, angle], shift_ref[1, angle]) * place, fine)
    turn = (3 * cycle - jnp.where(line == 0, 0, phase * fine)).astype(jnp.float32) / (3.0 * fine)
    turn = 2.0 * jnp.pi * turn
    cosine, sine = jnp.cos(turn), jnp.sin(turn)
    row_cos, row_sin = high_low(cosine[0:1]), high_low(sine[0:1])
    col_cos, col_sin = high_low((2.0 / 3.0) * cosine[1:2]), high_low((-2.0 / 3.0) * sine[1:2])
    third = high_low(jnp.full((1, fine), 1.0 / 3.0, jnp.float32))
    ones = jnp.ones((1, fine), jnp.bfloat16)
    left = [row_cos[0], row_cos[1], row_cos[0], row_sin[0], row_sin[1], row_sin[0], ones, ones]
    right = [col_cos[0], col_cos[0], col_cos[1], col_sin[0], col_sin[0], col_sin[1], third[0], third[1]]
    return jnp.concatenate(left, axis=0), jnp.concatenate(right, axis=0)


def filter_kernel(angle_hbm, phase_hbm, shift_hbm, raw_hbm, half_hbm, col_hbm, row_hbm, *refs):
    *out_refs, angle_ref, phase_ref, shift_ref, raw_ref, half_ref, col_ref, row_ref = refs[:-4]
    rows_ref, sum_ref, window_ref, arrived = refs[-4:]
    sources = (angle_hbm, phase_hbm, shift_hbm, raw_hbm, half_hbm, col_hbm, row_hbm)
    targets = (angle_ref, phase_ref, shift_ref, raw_ref, half_ref, col_ref, row_ref)
    copies = [
        pltpu.make_async_copy(source, target, arrived.at[i])
        for i, (source, target) in enumerate(zip(sources, targets))
    ]
    for copy in copies:
        copy.start()
    frames, coarse, _ = raw_ref.shape
    fine = 2 * coarse
    first = lax.axis_index("tm") * frames
    chip = lax.axis_index("tm") // 2
    for copy in copies[:3]:
        copy.wait()
    factors = [
        pattern_factors(angle_ref[first + f], phase_ref[first + f], shift_ref, fine) for f in range(frames)
    ]
    copies[3].wait()
    copies[4].wait()
    half_step = half_ref[...]
    for f in range(frames):
        rows_ref[f, :coarse] = raw_ref[f]
        rows_ref[f, coarse:] = dot(half_step, raw_ref[f]).astype(jnp.bfloat16)
    for r in range(0, fine, 2 * LANES):
        even, odd = 0.0, 0.0
        for f, (left, right) in enumerate(factors):
            rows_done = rows_ref[f, r:r + 2 * LANES]
            weight = dot(left[:, r:r + 2 * LANES], right, ((0,), (0,)))
            even += weight[:, :coarse] * rows_done.astype(jnp.float32)
            odd += weight[:, coarse:] * dot(rows_done, half_step, ((1,), (1,)))
        sum_ref[r:r + 2 * LANES, :coarse] = even.astype(jnp.bfloat16)
        sum_ref[r:r + 2 * LANES, coarse:] = odd.astype(jnp.bfloat16)
    copies[5].wait()
    filtered = dot(sum_ref[...], col_ref[...], ((1,), (1,))).astype(jnp.bfloat16)
    copies[6].wait()
    window_ref[...] = dot(row_ref[...], filtered).reshape(window_ref.shape).astype(jnp.bfloat16)
    for k, out_ref in enumerate(out_refs):
        out_ref[...] = window_ref[chip ^ k]


def on_core(core, rows, body):
    for c in range(2):
        @pl.when(core == c)
        def _(c=c):
            body(c * rows)


def partner_kernel(*refs):
    *in_refs, out_ref = refs
    rows = out_ref.shape[1]

    def take(start):
        for k, in_ref in enumerate(in_refs):
            out_ref[k] = in_ref[start:start + rows]

    on_core(1 - lax.axis_index("tm") % 2, rows - 2 * REACH, take)


def add(a, b):
    return [[x + y for x, y in zip(p, q)] for p, q in zip(a, b)]


def sub(a, b):
    return [[x - y for x, y in zip(p, q)] for p, q in zip(a, b)]


def times(a, factor):
    return [[x * factor for x in p] for p in a]


def by_row(a, factors):
    return [[x * f for x in p] for p, f in zip(a, factors)]


def clip(a, bound):
    return [[jnp.minimum(jnp.maximum(x, -bound), bound) for x in p] for p in a]


def ahead_y(a):
    return a[1:] + [[pltpu.roll(x, SUBLANES - 1, 0) for x in a[0]]]


def behind_y(a):
    return [[pltpu.roll(x, 1, 0) for x in a[-1]]] + a[:-1]


def ahead_x(a, last_lane):
    return [
        p[1:] + [jnp.where(last_lane, 0.0, pltpu.roll(p[0], LANES - 1, 1))] for p in a
    ]


def behind_x(a, first_lane, edge=None):
    return [
        [jnp.where(first_lane, 0.0 if edge is None else edge[j][0], pltpu.roll(p[-1], 1, 1))] + p[:-1]
        for j, p in enumerate(a)
    ]


def denoise_kernel(*refs, parts):
    *own_refs, early_ref, late_ref, order_ref, out_ref, window_ref = refs[:-12]
    partner_refs = [(k, ref, i) for part, ref in zip(parts, (early_ref, late_ref)) for i, k in enumerate(part)]
    denoise(window_ref, order_ref, out_ref, *refs[-12:], own_refs=own_refs, partner_refs=partner_refs)


def denoise(window_ref, order_ref, out_ref, guide_ref, first_ref, xx_ref, yy_ref, xy_ref, xt_ref, yt_ref, tt_ref,
                   past_ref, curve_ref, lines_ref, turned_ref, own_refs, partner_refs):
    count, rows, fine = window_ref.shape
    block_rows = rows - 2 * REACH
    major = rows // SUBLANES
    columns = fine // LANES
    tiles = [
        [(pl.ds(j * SUBLANES, SUBLANES), pl.ds(c * LANES, LANES)) for c in range(columns)] for j in range(major)
    ]
    lane = lax.broadcasted_iota(jnp.int32, (SUBLANES, LANES), 1)
    first_lane = lane == 0
    last_lane = lane == LANES - 1
    sublane = lax.broadcasted_iota(jnp.int32, (SUBLANES, LANES), 0)
    top_row = lax.axis_index("tm") * block_rows - REACH
    valid, twice_valid, twice_step = [], [], []
    for j in range(major):
        image_row = top_row + sublane * major + j
        inside = (image_row >= 0) & (image_row < fine)
        valid.append(jnp.where(inside, 1.0, 0.0))
        twice_valid.append(jnp.where(inside, 2.0, 0.0))
        twice_step.append(jnp.where(inside, 2.0 * STEP_SIZE, 0.0))

    def load(ref, t):
        return [[ref[(t, *tile)] for tile in line] for line in tiles]

    def store(ref, t, values):
        for line, p in zip(tiles, values):
            for tile, x in zip(line, p):
                ref[(t, *tile)] = x

    zero = [[jnp.zeros((SUBLANES, LANES), jnp.float32)] * columns] * major

    chip, core = lax.axis_index("tm") // 2, lax.axis_index("tm") % 2

    def place(start):
        for k, own_ref in enumerate(own_refs):
            window_ref[2 * (chip ^ k) + core] = own_ref[start:start + rows]

    on_core(core, block_rows, place)
    for k, partner_ref, i in partner_refs:
        window_ref[2 * (chip ^ k) + 1 - core] = partner_ref[i]

    def window(t):
        return [window_ref[t, :, pl.ds(c * LANES, LANES)].astype(jnp.float32) for c in range(columns)]

    def keep_sum(t, *frames):
        for c, parts in enumerate(zip(*[window(f) for f in frames])):
            lines_ref[c] = sum(parts[1:], parts[0])
            for j in range(major):
                guide_ref[t, pl.ds(j * SUBLANES, SUBLANES), pl.ds(c * LANES, LANES)] = lines_ref[
                    c, pl.ds(j, SUBLANES, stride=major), :
                ]

    def close(ref):
        store(ref, count, zero)
        store(ref, count + 1, times(load(ref, count - 1), -1.0))

    keep_sum(0, 0, 1)
    keep_sum(count - 1, count - 2, count - 1)
    close(guide_ref)

    def gather(t, carried):
        keep_sum(t, t - 1, t, t + 1)
        return carried

    lax.fori_loop(1, count - 1, gather, 0)

    def sweep(ref, finish, duals, before_pair=None):
        def settle(term, dual_ref, t, bound):
            if duals:
                return clip(add(term, load(dual_ref, t)), bound)
            fresh = clip(term, bound)
            store(dual_ref, t, fresh)
            return fresh

        def frame(t):
            here = load(ref, t)
            rise_x = sub(ahead_x(here, last_lane), here)
            fresh_xx = settle(sub(rise_x, behind_x(rise_x, first_lane, here)), xx_ref, t, THRESHOLD)
            flow_x = sub(ahead_x(fresh_xx, last_lane), fresh_xx)
            rise_y = sub(ahead_y(here), here)
            double_rise = by_row(rise_y, twice_valid)
            fresh_xy = settle(sub(ahead_x(double_rise, last_lane), double_rise), xy_ref, t, 2.0 * THRESHOLD)
            flow_x = add(flow_x, sub(fresh_xy, behind_y(fresh_xy)))
            total = sub(flow_x, behind_x(flow_x, first_lane, fresh_xx))

            curve_y = by_row(sub(rise_y, behind_y(rise_y)), valid)
            fresh_yy = settle(curve_y, yy_ref, t, THRESHOLD)
            flow_y = sub(ahead_y(fresh_yy), fresh_yy)
            total = add(total, sub(flow_y, behind_y(flow_y)))

            after = load(ref, t + 1)
            rise_t = sub(after, here)
            twice_t = times(rise_t, 2.0)
            fresh_xt = settle(sub(ahead_x(twice_t, last_lane), twice_t), xt_ref, t, 2.0 * THRESHOLD)
            bend = by_row(sub(ahead_y(rise_t), rise_t), twice_valid)
            fresh_yt = settle(bend, yt_ref, t, 2.0 * THRESHOLD)
            flow_t = add(sub(fresh_xt, behind_x(fresh_xt, first_lane)), sub(fresh_yt, behind_y(fresh_yt)))
            next_tt = settle(sub(sub(load(ref, t + 2), after), rise_t), tt_ref, t + 1, THRESHOLD)
            flow_t = add(flow_t, sub(next_tt, load(curve_ref, 0)))
            total = add(total, sub(flow_t, load(past_ref, 0)))
            store(past_ref, 0, flow_t)
            store(curve_ref, 0, next_tt)
            finish(t, here, total)

        def pair(k, carried):
            if before_pair is not None:
                before_pair(jnp.maximum(k - 1, 0))
            frame(2 * k)
            frame(2 * k + 1)
            return carried

        start = load(ref, 0)
        first_tt = settle(sub(sub(load(ref, 1), start), start), tt_ref, 0, THRESHOLD)
        store(curve_ref, 0, first_tt)
        store(past_ref, 0, first_tt)
        lax.fori_loop(0, count // 2, pair, 0)

    def finish_first(t, here, total):
        store(first_ref, t, sub(here, by_row(total, twice_step)))

    def finish_last(t, here, total):
        change = sub(load(guide_ref, t), here)
        update = sub(add(here, times(change, STEP_SIZE + 0.5)), times(total, 2.0 * STEP_SIZE))
        slot = lax.rem(t, 2) * block_rows
        for c in range(columns):
            for j in range(major):
                lines_ref[c, pl.ds(j, SUBLANES, stride=major), :] = update[j][c]
            high, low = high_low(lines_ref[c, pl.ds(REACH, block_rows), :])
            turned_ref[pl.ds(slot, block_rows), pl.ds(c * LANES, LANES)] = high
            turned_ref[pl.ds(2 * block_rows + slot, block_rows), pl.ds(c * LANES, LANES)] = low

    def reorder(k):
        both = dot(turned_ref[...], order_ref[...])
        both = both[:2 * block_rows] + both[2 * block_rows:]
        out_ref[pl.ds(2 * k, 2)] = both.reshape(2, block_rows, fine)

    sweep(guide_ref, finish_first, False)
    close(first_ref)
    turned_ref[...] = jnp.zeros_like(turned_ref)
    sweep(first_ref, finish_last, True, reorder)
    reorder(count // 2 - 1)


def shards(raw_frames, angle_index, phase_index, band_shift):
    raw_count, coarse, _ = raw_frames.shape
    fine = 2 * coarse
    tm_count = lax.axis_size("tm")
    chips = tm_count // 2
    block_rows = fine // tm_count
    window_rows = block_rows + 2 * REACH
    chip_rows = 2 * block_rows + 2 * REACH
    wiener = wiener_table(fine)
    half_step = half_table(coarse)
    col_filter = wiener[columns_of(fine)][:, split_order(fine)]
    row_windows = row_filter(wiener, chips, 2 * block_rows)
    order = np.eye(fine, dtype=jnp.bfloat16)[columns_of(fine)]
    sources = (angle_index, phase_index, band_shift.T, raw_frames, half_step, col_filter, row_windows)
    vector = pl.BlockSpec(memory_space=pltpu.VMEM)
    frames = pl.pallas_call(
        filter_kernel,
        out_shape=[jax.ShapeDtypeStruct((chip_rows, fine), jnp.bfloat16)] * chips,
        in_specs=[pl.BlockSpec(memory_space=pltpu.HBM)] * len(sources),
        out_specs=[vector] * chips,
        scratch_shapes=[
            *[pltpu.SMEM(v.shape, v.dtype) for v in sources[:3]],
            *[pltpu.VMEM(v.shape, v.dtype) for v in sources[3:]],
            pltpu.VMEM((raw_count, fine, coarse), jnp.bfloat16), pltpu.VMEM((fine, fine), jnp.bfloat16),
            pltpu.VMEM((chips, chip_rows, fine), jnp.bfloat16), pltpu.SemaphoreType.DMA((len(sources),)),
        ],
        name="filter_group",
    )(*sources)
    received = list(frames)
    for k in reversed(exchange_order(chips)):
        received[k] = lax.ppermute(frames[k], "tm", [(i, i ^ (2 * k)) for i in range(tm_count)])
    half = chips // 2
    early = [0] + exchange_order(chips)[:half - 1]
    late = [k for k in range(chips) if k not in early]
    partner = [
        pl.pallas_call(
            partner_kernel,
            out_shape=jax.ShapeDtypeStruct((half, window_rows, fine), jnp.bfloat16),
            in_specs=[vector] * half,
            out_specs=vector,
            compiler_params=pltpu.CompilerParams(vmem_limit_bytes=8 << 20),
            name="partner_rows",
        )(*[received[k] for k in part])
        for part in (early, late)
    ]
    partner = [lax.ppermute(v, "tm", [(i, i ^ 1) for i in range(tm_count)]) for v in partner]

    def field(frames):
        return pltpu.VMEM((frames, window_rows, fine), jnp.float32)

    return pl.pallas_call(
        partial(denoise_kernel, parts=(early, late)),
        out_shape=jax.ShapeDtypeStruct((tm_count, block_rows, fine), jnp.float32),
        in_specs=[vector] * (chips + 3),
        out_specs=vector,
        scratch_shapes=[
            pltpu.VMEM((tm_count, window_rows, fine), jnp.bfloat16),
            field(tm_count + 2), field(tm_count + 2), *[field(tm_count)] * 5, field(tm_count + 1),
            field(1), field(1), pltpu.VMEM((fine // LANES, window_rows, LANES), jnp.float32),
            pltpu.VMEM((4 * block_rows, fine), jnp.bfloat16),
        ],
        compiler_params=pltpu.CompilerParams(vmem_limit_bytes=40 << 20),
        name="denoise_rows",
    )(*received, *partner, order)


def solution(mesh):
    return jax.shard_map(
        shards,
        mesh=mesh,
        in_specs=(P(("grp", "tm"), None, None), P("grp"), P("grp"), P("grp", None)),
        out_specs=P("grp", "tm", None),
        check_vma=False,
    )
```

```python
from functools import partial

import jax
import jax.numpy as jnp
import numpy as np
from jax import lax
from jax.experimental import pallas as pl
from jax.experimental.pallas import tpu as pltpu
from jax.sharding import PartitionSpec as P

SWEEPS = 2
STEP_SIZE = 0.01
THRESHOLD = 2.0
REACH = 2 * SWEEPS
LANES = 128
SUBLANES = 8


def half_table(coarse):
    offset = np.arange(coarse)[:, None] - np.arange(coarse)[None, :]
    parity = (1.0 - 2.0 * (offset % 2)).astype(np.float32)
    angle_arg = np.float32(np.pi) * (offset.astype(np.float32) + np.float32(0.5)) / np.float32(coarse)
    return (parity / (np.float32(coarse) * np.tan(angle_arg))).astype(jnp.bfloat16)


def wiener_table(width):
    distance = np.abs(np.arange(width)[:, None] - np.arange(width)[None, :])
    distance = np.minimum(distance, width - distance)
    taps = np.float32(-0.01) * np.power(np.float32(0.98), (distance - 1).astype(np.float32))
    return np.where(distance == 0, np.float32(1.0), taps).astype(jnp.bfloat16)


def split_order(width):
    return np.concatenate([np.arange(0, width, 2), np.arange(1, width, 2)])


def columns_of(fine):
    stored = np.arange(fine)
    return (stored % LANES) * (fine // LANES) + stored // LANES


def row_filter(wiener, blocks, block_rows):
    fine = wiener.shape[0]
    row = np.arange(blocks)[:, None] * block_rows + np.arange(-REACH, block_rows + REACH)[None, :]
    valid = (row >= 0) & (row < fine)
    table = wiener[np.clip(row, 0, fine - 1)][:, :, split_order(fine)]
    return np.where(valid[:, :, None], table, np.zeros((), jnp.bfloat16)).reshape(-1, fine)


def exchange_order(chips):
    head = [chips // 2, chips // 2 + 1, chips // 2 - 1]
    return head + [k for k in reversed(range(1, chips)) if k not in head]


def dot(a, b, dims=((1,), (0,))):
    return lax.dot_general(a, b, (dims, ((), ())), preferred_element_type=jnp.float32)


def high_low(value):
    high = value.astype(jnp.bfloat16)
    return high, (value - high.astype(jnp.float32)).astype(jnp.bfloat16)


def pattern_factors(angle, phase, shift_ref, fine):
    lane = lax.broadcasted_iota(jnp.int32, (SUBLANES, fine), 1)
    line = lax.broadcasted_iota(jnp.int32, (SUBLANES, fine), 0)
    place = jnp.where(lane < fine // 2, 2 * lane, 2 * lane - fine + 1)
    cycle = lax.rem(jnp.where(line == 0, shift_ref[0, angle], shift_ref[1, angle]) * place, fine)
    turn = (3 * cycle - jnp.where(line == 0, 0, phase * fine)).astype(jnp.float32) / (3.0 * fine)
    turn = 2.0 * jnp.pi * turn
    cosine, sine = jnp.cos(turn), jnp.sin(turn)
    row_cos, row_sin = high_low(cosine[0:1]), high_low(sine[0:1])
    col_cos, col_sin = high_low((2.0 / 3.0) * cosine[1:2]), high_low((-2.0 / 3.0) * sine[1:2])
    third = high_low(jnp.full((1, fine), 1.0 / 3.0, jnp.float32))
    ones = jnp.ones((1, fine), jnp.bfloat16)
    left = [row_cos[0], row_cos[1], row_cos[0], row_sin[0], row_sin[1], row_sin[0], ones, ones]
    right = [col_cos[0], col_cos[0], col_cos[1], col_sin[0], col_sin[0], col_sin[1], third[0], third[1]]
    return jnp.concatenate(left, axis=0), jnp.concatenate(right, axis=0)


def filter_kernel(angle_hbm, phase_hbm, shift_hbm, raw_hbm, half_hbm, col_hbm, row_hbm, *refs):
    *out_refs, angle_ref, phase_ref, shift_ref, raw_ref, half_ref, col_ref, row_ref = refs[:-4]
    rows_ref, sum_ref, window_ref, arrived = refs[-4:]
    sources = (angle_hbm, phase_hbm, shift_hbm, raw_hbm, half_hbm, col_hbm, row_hbm)
    targets = (angle_ref, phase_ref, shift_ref, raw_ref, half_ref, col_ref, row_ref)
    copies = [
        pltpu.make_async_copy(source, target, arrived.at[i])
        for i, (source, target) in enumerate(zip(sources, targets))
    ]
    for copy in copies:
        copy.start()
    frames, coarse, _ = raw_ref.shape
    fine = 2 * coarse
    first = lax.axis_index("tm") * frames
    chip = lax.axis_index("tm") // 2
    for copy in copies[:3]:
        copy.wait()
    factors = [
        pattern_factors(angle_ref[first + f], phase_ref[first + f], shift_ref, fine) for f in range(frames)
    ]
    copies[3].wait()
    copies[4].wait()
    half_step = half_ref[...]
    for f in range(frames):
        rows_ref[f, :coarse] = raw_ref[f]
        rows_ref[f, coarse:] = dot(half_step, raw_ref[f]).astype(jnp.bfloat16)
    for r in range(0, fine, 2 * LANES):
        even, odd = 0.0, 0.0
        for f, (left, right) in enumerate(factors):
            rows_done = rows_ref[f, r:r + 2 * LANES]
            weight = dot(left[:, r:r + 2 * LANES], right, ((0,), (0,)))
            even += weight[:, :coarse] * rows_done.astype(jnp.float32)
            odd += weight[:, coarse:] * dot(rows_done, half_step, ((1,), (1,)))
        sum_ref[r:r + 2 * LANES, :coarse] = even.astype(jnp.bfloat16)
        sum_ref[r:r + 2 * LANES, coarse:] = odd.astype(jnp.bfloat16)
    copies[5].wait()
    filtered = dot(sum_ref[...], col_ref[...], ((1,), (1,))).astype(jnp.bfloat16)
    copies[6].wait()
    window_ref[...] = dot(row_ref[...], filtered).reshape(window_ref.shape).astype(jnp.bfloat16)
    for k, out_ref in enumerate(out_refs):
        out_ref[...] = window_ref[chip ^ k]


def on_core(core, rows, body):
    for c in range(2):
        @pl.when(core == c)
        def _(c=c):
            body(c * rows)


def partner_kernel(*refs):
    *in_refs, out_ref = refs
    rows = out_ref.shape[1]

    def take(start):
        for k, in_ref in enumerate(in_refs):
            out_ref[k] = in_ref[start:start + rows]

    on_core(1 - lax.axis_index("tm") % 2, rows - 2 * REACH, take)


def add(a, b):
    return [[x + y for x, y in zip(p, q)] for p, q in zip(a, b)]


def sub(a, b):
    return [[x - y for x, y in zip(p, q)] for p, q in zip(a, b)]


def times(a, factor):
    return [[x * factor for x in p] for p in a]


def by_row(a, factors):
    return [[x * f for x in p] for p, f in zip(a, factors)]


def clip(a, bound):
    return [[jnp.minimum(jnp.maximum(x, -bound), bound) for x in p] for p in a]


def ahead_y(a):
    return a[1:] + [[pltpu.roll(x, SUBLANES - 1, 0) for x in a[0]]]


def behind_y(a):
    return [[pltpu.roll(x, 1, 0) for x in a[-1]]] + a[:-1]


def ahead_x(a, last_lane):
    return [
        p[1:] + [jnp.where(last_lane, 0.0, pltpu.roll(p[0], LANES - 1, 1))] for p in a
    ]


def behind_x(a, first_lane, edge=None):
    return [
        [jnp.where(first_lane, 0.0 if edge is None else edge[j][0], pltpu.roll(p[-1], 1, 1))] + p[:-1]
        for j, p in enumerate(a)
    ]


def denoise_kernel(*refs, offsets):
    *own_refs, early_ref, late_ref, order_ref, out_ref, window_ref = refs[:-12]
    partner_refs = [ref.at[i] for ref in (early_ref, late_ref) for i in range(ref.shape[0])]
    denoise(window_ref, order_ref, out_ref, *refs[-12:], offsets, own_refs, partner_refs)


def denoise(window_ref, order_ref, out_ref, guide_ref, first_ref, xx_ref, yy_ref, xy_ref, xt_ref, yt_ref, tt_ref,
                   past_ref, curve_ref, lines_ref, turned_ref, offsets, own_refs, partner_refs):
    count, rows, fine = window_ref.shape
    block_rows = rows - 2 * REACH
    major = rows // SUBLANES
    columns = fine // LANES
    tiles = [
        [(pl.ds(j * SUBLANES, SUBLANES), pl.ds(c * LANES, LANES)) for c in range(columns)] for j in range(major)
    ]
    lane = lax.broadcasted_iota(jnp.int32, (SUBLANES, LANES), 1)
    first_lane = lane == 0
    last_lane = lane == LANES - 1
    sublane = lax.broadcasted_iota(jnp.int32, (SUBLANES, LANES), 0)
    top_row = lax.axis_index("tm") * block_rows - REACH
    valid, twice_valid, twice_step = [], [], []
    for j in range(major):
        image_row = top_row + sublane * major + j
        inside = (image_row >= 0) & (image_row < fine)
        valid.append(jnp.where(inside, 1.0, 0.0))
        twice_valid.append(jnp.where(inside, 2.0, 0.0))
        twice_step.append(jnp.where(inside, 2.0 * STEP_SIZE, 0.0))

    def load(ref, t):
        return [[ref[(t, *tile)] for tile in line] for line in tiles]

    def store(ref, t, values):
        for line, p in zip(tiles, values):
            for tile, x in zip(line, p):
                ref[(t, *tile)] = x

    zero = [[jnp.zeros((SUBLANES, LANES), jnp.float32)] * columns] * major

    chip, core = lax.axis_index("tm") // 2, lax.axis_index("tm") % 2

    def place(start):
        for k, own_ref in zip(offsets, own_refs):
            window_ref[2 * (chip ^ k) + core] = own_ref[start:start + rows]

    on_core(core, block_rows, place)
    for k, partner_ref in zip(offsets, partner_refs):
        window_ref[2 * (chip ^ k) + 1 - core] = partner_ref[...]

    def window(t):
        return [window_ref[t, :, pl.ds(c * LANES, LANES)].astype(jnp.float32) for c in range(columns)]

    def keep_sum(t, *frames):
        for c, parts in enumerate(zip(*[window(f) for f in frames])):
            lines_ref[c] = sum(parts[1:], parts[0])
            for j in range(major):
                guide_ref[t, pl.ds(j * SUBLANES, SUBLANES), pl.ds(c * LANES, LANES)] = lines_ref[
                    c, pl.ds(j, SUBLANES, stride=major), :
                ]

    def close(ref):
        store(ref, count, zero)
        store(ref, count + 1, times(load(ref, count - 1), -1.0))

    keep_sum(0, 0, 1)
    keep_sum(count - 1, count - 2, count - 1)
    close(guide_ref)

    def gather(t, carried):
        keep_sum(t, t - 1, t, t + 1)
        return carried

    lax.fori_loop(1, count - 1, gather, 0)

    def sweep(ref, finish, duals, before_pair=None):
        def settle(term, dual_ref, t, bound):
            if duals:
                return clip(add(term, load(dual_ref, t)), bound)
            fresh = clip(term, bound)
            store(dual_ref, t, fresh)
            return fresh

        def frame(t):
            here = load(ref, t)
            rise_x = sub(ahead_x(here, last_lane), here)
            fresh_xx = settle(sub(rise_x, behind_x(rise_x, first_lane, here)), xx_ref, t, THRESHOLD)
            flow_x = sub(ahead_x(fresh_xx, last_lane), fresh_xx)
            rise_y = sub(ahead_y(here), here)
            double_rise = by_row(rise_y, twice_valid)
            fresh_xy = settle(sub(ahead_x(double_rise, last_lane), double_rise), xy_ref, t, 2.0 * THRESHOLD)
            flow_x = add(flow_x, sub(fresh_xy, behind_y(fresh_xy)))
            total = sub(flow_x, behind_x(flow_x, first_lane, fresh_xx))

            curve_y = by_row(sub(rise_y, behind_y(rise_y)), valid)
            fresh_yy = settle(curve_y, yy_ref, t, THRESHOLD)
            flow_y = sub(ahead_y(fresh_yy), fresh_yy)
            total = add(total, sub(flow_y, behind_y(flow_y)))

            after = load(ref, t + 1)
            rise_t = sub(after, here)
            twice_t = times(rise_t, 2.0)
            fresh_xt = settle(sub(ahead_x(twice_t, last_lane), twice_t), xt_ref, t, 2.0 * THRESHOLD)
            bend = by_row(sub(ahead_y(rise_t), rise_t), twice_valid)
            fresh_yt = settle(bend, yt_ref, t, 2.0 * THRESHOLD)
            flow_t = add(sub(fresh_xt, behind_x(fresh_xt, first_lane)), sub(fresh_yt, behind_y(fresh_yt)))
            next_tt = settle(sub(sub(load(ref, t + 2), after), rise_t), tt_ref, t + 1, THRESHOLD)
            flow_t = add(flow_t, sub(next_tt, load(curve_ref, 0)))
            total = add(total, sub(flow_t, load(past_ref, 0)))
            store(past_ref, 0, flow_t)
            store(curve_ref, 0, next_tt)
            finish(t, here, total)

        def pair(k, carried):
            if before_pair is not None:
                before_pair(jnp.maximum(k - 1, 0))
            frame(2 * k)
            frame(2 * k + 1)
            return carried

        start = load(ref, 0)
        first_tt = settle(sub(sub(load(ref, 1), start), start), tt_ref, 0, THRESHOLD)
        store(curve_ref, 0, first_tt)
        store(past_ref, 0, first_tt)
        lax.fori_loop(0, count // 2, pair, 0)

    def finish_first(t, here, total):
        store(first_ref, t, sub(here, by_row(total, twice_step)))

    def finish_last(t, here, total):
        change = sub(load(guide_ref, t), here)
        update = sub(add(here, times(change, STEP_SIZE + 0.5)), times(total, 2.0 * STEP_SIZE))
        slot = lax.rem(t, 2) * block_rows
        for c in range(columns):
            for j in range(major):
                lines_ref[c, pl.ds(j, SUBLANES, stride=major), :] = update[j][c]
            high, low = high_low(lines_ref[c, pl.ds(REACH, block_rows), :])
            turned_ref[pl.ds(slot, block_rows), pl.ds(c * LANES, LANES)] = high
            turned_ref[pl.ds(2 * block_rows + slot, block_rows), pl.ds(c * LANES, LANES)] = low

    def reorder(k):
        both = dot(turned_ref[...], order_ref[...])
        both = both[:2 * block_rows] + both[2 * block_rows:]
        out_ref[pl.ds(2 * k, 2)] = both.reshape(2, block_rows, fine)

    sweep(guide_ref, finish_first, False)
    close(first_ref)
    turned_ref[...] = jnp.zeros_like(turned_ref)
    sweep(first_ref, finish_last, True, reorder)
    reorder(count // 2 - 1)


def shards(raw_frames, angle_index, phase_index, band_shift):
    raw_count, coarse, _ = raw_frames.shape
    fine = 2 * coarse
    tm_count = lax.axis_size("tm")
    chips = tm_count // 2
    block_rows = fine // tm_count
    window_rows = block_rows + 2 * REACH
    chip_rows = 2 * block_rows + 2 * REACH
    wiener = wiener_table(fine)
    half_step = half_table(coarse)
    col_filter = wiener[columns_of(fine)][:, split_order(fine)]
    row_windows = row_filter(wiener, chips, 2 * block_rows)
    order = np.eye(fine, dtype=jnp.bfloat16)[columns_of(fine)]
    sources = (angle_index, phase_index, band_shift.T, raw_frames, half_step, col_filter, row_windows)
    vector = pl.BlockSpec(memory_space=pltpu.VMEM)
    frames = pl.pallas_call(
        filter_kernel,
        out_shape=[jax.ShapeDtypeStruct((chip_rows, fine), jnp.bfloat16)] * chips,
        in_specs=[pl.BlockSpec(memory_space=pltpu.HBM)] * len(sources),
        out_specs=[vector] * chips,
        scratch_shapes=[
            *[pltpu.SMEM(v.shape, v.dtype) for v in sources[:3]],
            *[pltpu.VMEM(v.shape, v.dtype) for v in sources[3:]],
            pltpu.VMEM((raw_count, fine, coarse), jnp.bfloat16), pltpu.VMEM((fine, fine), jnp.bfloat16),
            pltpu.VMEM((chips, chip_rows, fine), jnp.bfloat16), pltpu.SemaphoreType.DMA((len(sources),)),
        ],
        name="filter_group",
    )(*sources)
    offsets = [0] + exchange_order(chips)
    received = [frames[0]]
    for k in offsets[1:]:
        received.append(lax.ppermute(frames[k], "tm", [(i, i ^ (2 * k)) for i in range(tm_count)]))
    half = chips // 2
    partner = [
        pl.pallas_call(
            partner_kernel,
            out_shape=jax.ShapeDtypeStruct((half, window_rows, fine), jnp.bfloat16),
            in_specs=[vector] * half,
            out_specs=vector,
            compiler_params=pltpu.CompilerParams(vmem_limit_bytes=8 << 20),
            name="partner_rows",
        )(*part)
        for part in (received[:half], received[half:])
    ]
    partner = [lax.ppermute(v, "tm", [(i, i ^ 1) for i in range(tm_count)]) for v in partner]

    def field(frames):
        return pltpu.VMEM((frames, window_rows, fine), jnp.float32)

    return pl.pallas_call(
        partial(denoise_kernel, offsets=offsets),
        out_shape=jax.ShapeDtypeStruct((tm_count, block_rows, fine), jnp.float32),
        in_specs=[vector] * (chips + 3),
        out_specs=vector,
        scratch_shapes=[
            pltpu.VMEM((tm_count, window_rows, fine), jnp.bfloat16),
            field(tm_count + 2), field(tm_count + 2), *[field(tm_count)] * 5, field(tm_count + 1),
            field(1), field(1), pltpu.VMEM((fine // LANES, window_rows, LANES), jnp.float32),
            pltpu.VMEM((4 * block_rows, fine), jnp.bfloat16),
        ],
        compiler_params=pltpu.CompilerParams(vmem_limit_bytes=40 << 20),
        name="denoise_rows",
    )(*received, *partner, order)


def solution(mesh):
    return jax.shard_map(
        shards,
        mesh=mesh,
        in_specs=(P(("grp", "tm"), None, None), P("grp"), P("grp"), P("grp", None)),
        out_specs=P("grp", "tm", None),
        check_vma=False,
    )
```

```python
from functools import partial

import jax
import jax.numpy as jnp
import numpy as np
from jax import lax
from jax.experimental import pallas as pl
from jax.experimental.pallas import tpu as pltpu
from jax.sharding import PartitionSpec as P

SWEEPS = 2
STEP_SIZE = 0.01
THRESHOLD = 2.0
REACH = 2 * SWEEPS
LANES = 128
SUBLANES = 8


def half_table(coarse):
    offset = np.arange(coarse)[:, None] - np.arange(coarse)[None, :]
    parity = (1.0 - 2.0 * (offset % 2)).astype(np.float32)
    angle_arg = np.float32(np.pi) * (offset.astype(np.float32) + np.float32(0.5)) / np.float32(coarse)
    return (parity / (np.float32(coarse) * np.tan(angle_arg))).astype(jnp.bfloat16)


def wiener_table(width):
    distance = np.abs(np.arange(width)[:, None] - np.arange(width)[None, :])
    distance = np.minimum(distance, width - distance)
    taps = np.float32(-0.01) * np.power(np.float32(0.98), (distance - 1).astype(np.float32))
    return np.where(distance == 0, np.float32(1.0), taps).astype(jnp.bfloat16)


def split_order(width):
    return np.concatenate([np.arange(0, width, 2), np.arange(1, width, 2)])


def columns_of(fine):
    stored = np.arange(fine)
    return (stored % LANES) * (fine // LANES) + stored // LANES


def row_filter(wiener, blocks, block_rows):
    fine = wiener.shape[0]
    row = np.arange(blocks)[:, None] * block_rows + np.arange(-REACH, block_rows + REACH)[None, :]
    valid = (row >= 0) & (row < fine)
    table = wiener[np.clip(row, 0, fine - 1)][:, :, split_order(fine)]
    return np.where(valid[:, :, None], table, np.zeros((), jnp.bfloat16)).reshape(-1, fine)


def exchange_order(chips):
    head = [chips // 2, chips // 2 + 1, chips // 2 - 1]
    return head + [k for k in reversed(range(1, chips)) if k not in head]


def dot(a, b, dims=((1,), (0,))):
    return lax.dot_general(a, b, (dims, ((), ())), preferred_element_type=jnp.float32)


def high_low(value):
    high = value.astype(jnp.bfloat16)
    return high, (value - high.astype(jnp.float32)).astype(jnp.bfloat16)


def pattern_factors(angle, phase, shift_ref, fine):
    lane = lax.broadcasted_iota(jnp.int32, (SUBLANES, fine), 1)
    line = lax.broadcasted_iota(jnp.int32, (SUBLANES, fine), 0)
    place = jnp.where(lane < fine // 2, 2 * lane, 2 * lane - fine + 1)
    cycle = lax.rem(jnp.where(line == 0, shift_ref[0, angle], shift_ref[1, angle]) * place, fine)
    turn = (3 * cycle - jnp.where(line == 0, 0, phase * fine)).astype(jnp.float32) / (3.0 * fine)
    turn = 2.0 * jnp.pi * turn
    cosine, sine = jnp.cos(turn), jnp.sin(turn)
    row_cos, row_sin = high_low(cosine[0:1]), high_low(sine[0:1])
    col_cos, col_sin = high_low((2.0 / 3.0) * cosine[1:2]), high_low((-2.0 / 3.0) * sine[1:2])
    third = high_low(jnp.full((1, fine), 1.0 / 3.0, jnp.float32))
    ones = jnp.ones((1, fine), jnp.bfloat16)
    left = [row_cos[0], row_cos[1], row_cos[0], row_sin[0], row_sin[1], row_sin[0], ones, ones]
    right = [col_cos[0], col_cos[0], col_cos[1], col_sin[0], col_sin[0], col_sin[1], third[0], third[1]]
    return jnp.concatenate(left, axis=0), jnp.concatenate(right, axis=0)


def filter_kernel(angle_hbm, phase_hbm, shift_hbm, raw_hbm, half_hbm, col_hbm, row_hbm, *refs):
    *out_refs, angle_ref, phase_ref, shift_ref, raw_ref, half_ref, col_ref, row_ref = refs[:-4]
    rows_ref, sum_ref, window_ref, arrived = refs[-4:]
    sources = (angle_hbm, phase_hbm, shift_hbm, raw_hbm, half_hbm, col_hbm, row_hbm)
    targets = (angle_ref, phase_ref, shift_ref, raw_ref, half_ref, col_ref, row_ref)
    copies = [
        pltpu.make_async_copy(source, target, arrived.at[i])
        for i, (source, target) in enumerate(zip(sources, targets))
    ]
    for copy in copies:
        copy.start()
    frames, coarse, _ = raw_ref.shape
    fine = 2 * coarse
    first = lax.axis_index("tm") * frames
    chip = lax.axis_index("tm") // 2
    for copy in copies[:3]:
        copy.wait()
    factors = [
        pattern_factors(angle_ref[first + f], phase_ref[first + f], shift_ref, fine) for f in range(frames)
    ]
    copies[3].wait()
    copies[4].wait()
    half_step = half_ref[...]
    for f in range(frames):
        rows_ref[f, :coarse] = raw_ref[f]
        rows_ref[f, coarse:] = dot(half_step, raw_ref[f]).astype(jnp.bfloat16)
    for r in range(0, fine, 2 * LANES):
        even, odd = 0.0, 0.0
        for f, (left, right) in enumerate(factors):
            rows_done = rows_ref[f, r:r + 2 * LANES]
            weight = dot(left[:, r:r + 2 * LANES], right, ((0,), (0,)))
            even += weight[:, :coarse] * rows_done.astype(jnp.float32)
            odd += weight[:, coarse:] * dot(rows_done, half_step, ((1,), (1,)))
        sum_ref[r:r + 2 * LANES, :coarse] = even.astype(jnp.bfloat16)
        sum_ref[r:r + 2 * LANES, coarse:] = odd.astype(jnp.bfloat16)
    copies[5].wait()
    filtered = dot(sum_ref[...], col_ref[...], ((1,), (1,))).astype(jnp.bfloat16)
    copies[6].wait()
    window_ref[...] = dot(row_ref[...], filtered).reshape(window_ref.shape).astype(jnp.bfloat16)
    for k, out_ref in enumerate(out_refs):
        out_ref[...] = window_ref[chip ^ k]


def on_core(core, rows, body):
    for c in range(2):
        @pl.when(core == c)
        def _(c=c):
            body(c * rows)


def partner_kernel(*refs):
    *in_refs, out_ref = refs
    rows = out_ref.shape[1]

    def take(start):
        for k, in_ref in enumerate(in_refs):
            out_ref[k] = in_ref[start:start + rows]

    on_core(1 - lax.axis_index("tm") % 2, rows - 2 * REACH, take)


def add(a, b):
    return [[x + y for x, y in zip(p, q)] for p, q in zip(a, b)]


def sub(a, b):
    return [[x - y for x, y in zip(p, q)] for p, q in zip(a, b)]


def times(a, factor):
    return [[x * factor for x in p] for p in a]


def by_row(a, factors):
    return [[x * f for x in p] for p, f in zip(a, factors)]


def clip(a, bound):
    return [[jnp.minimum(jnp.maximum(x, -bound), bound) for x in p] for p in a]


def ahead_y(a):
    return a[1:] + [[pltpu.roll(x, SUBLANES - 1, 0) for x in a[0]]]


def behind_y(a):
    return [[pltpu.roll(x, 1, 0) for x in a[-1]]] + a[:-1]


def ahead_x(a, last_lane):
    return [
        p[1:] + [jnp.where(last_lane, 0.0, pltpu.roll(p[0], LANES - 1, 1))] for p in a
    ]


def behind_x(a, first_lane, edge=None):
    return [
        [jnp.where(first_lane, 0.0 if edge is None else edge[j][0], pltpu.roll(p[-1], 1, 1))] + p[:-1]
        for j, p in enumerate(a)
    ]


def denoise_kernel(*refs, offsets):
    *own_refs, early_ref, late_ref, order_ref, out_ref, window_ref = refs[:-14]
    partner_refs = [ref.at[i] for ref in (early_ref, late_ref) for i in range(ref.shape[0])]
    denoise(window_ref, order_ref, out_ref, *refs[-14:], offsets, own_refs, partner_refs)


def denoise(window_ref, order_ref, out_ref, guide_ref, first_ref, xx_ref, yy_ref, xy_ref, xt_ref, yt_ref, tt_ref,
                   past_ref, curve_ref, lines_ref, turned_ref, done_ref, sent, offsets, own_refs, partner_refs):
    count, rows, fine = window_ref.shape
    block_rows = rows - 2 * REACH
    major = rows // SUBLANES
    columns = fine // LANES
    tiles = [
        [(pl.ds(j * SUBLANES, SUBLANES), pl.ds(c * LANES, LANES)) for c in range(columns)] for j in range(major)
    ]
    lane = lax.broadcasted_iota(jnp.int32, (SUBLANES, LANES), 1)
    first_lane = lane == 0
    last_lane = lane == LANES - 1
    sublane = lax.broadcasted_iota(jnp.int32, (SUBLANES, LANES), 0)
    top_row = lax.axis_index("tm") * block_rows - REACH
    valid, twice_valid, twice_step = [], [], []
    for j in range(major):
        image_row = top_row + sublane * major + j
        inside = (image_row >= 0) & (image_row < fine)
        valid.append(jnp.where(inside, 1.0, 0.0))
        twice_valid.append(jnp.where(inside, 2.0, 0.0))
        twice_step.append(jnp.where(inside, 2.0 * STEP_SIZE, 0.0))

    def load(ref, t):
        return [[ref[(t, *tile)] for tile in line] for line in tiles]

    def store(ref, t, values):
        for line, p in zip(tiles, values):
            for tile, x in zip(line, p):
                ref[(t, *tile)] = x

    zero = [[jnp.zeros((SUBLANES, LANES), jnp.float32)] * columns] * major

    chip, core = lax.axis_index("tm") // 2, lax.axis_index("tm") % 2

    def place(start):
        for k, own_ref in zip(offsets, own_refs):
            window_ref[2 * (chip ^ k) + core] = own_ref[start:start + rows]

    on_core(core, block_rows, place)
    for k, partner_ref in zip(offsets, partner_refs):
        window_ref[2 * (chip ^ k) + 1 - core] = partner_ref[...]

    def window(t):
        return [window_ref[t, :, pl.ds(c * LANES, LANES)].astype(jnp.float32) for c in range(columns)]

    def keep_sum(t, *frames):
        for c, parts in enumerate(zip(*[window(f) for f in frames])):
            lines_ref[c] = sum(parts[1:], parts[0])
            for j in range(major):
                guide_ref[t, pl.ds(j * SUBLANES, SUBLANES), pl.ds(c * LANES, LANES)] = lines_ref[
                    c, pl.ds(j, SUBLANES, stride=major), :
                ]

    def close(ref):
        store(ref, count, zero)
        store(ref, count + 1, times(load(ref, count - 1), -1.0))

    keep_sum(0, 0, 1)
    keep_sum(count - 1, count - 2, count - 1)
    close(guide_ref)

    def gather(t, carried):
        keep_sum(t, t - 1, t, t + 1)
        return carried

    lax.fori_loop(1, count - 1, gather, 0)

    def sweep(ref, finish, duals, before_pair=None, after_pair=None):
        def settle(term, dual_ref, t, bound):
            if duals:
                return clip(add(term, load(dual_ref, t)), bound)
            fresh = clip(term, bound)
            store(dual_ref, t, fresh)
            return fresh

        def frame(t):
            here = load(ref, t)
            rise_x = sub(ahead_x(here, last_lane), here)
            fresh_xx = settle(sub(rise_x, behind_x(rise_x, first_lane, here)), xx_ref, t, THRESHOLD)
            flow_x = sub(ahead_x(fresh_xx, last_lane), fresh_xx)
            rise_y = sub(ahead_y(here), here)
            double_rise = by_row(rise_y, twice_valid)
            fresh_xy = settle(sub(ahead_x(double_rise, last_lane), double_rise), xy_ref, t, 2.0 * THRESHOLD)
            flow_x = add(flow_x, sub(fresh_xy, behind_y(fresh_xy)))
            total = sub(flow_x, behind_x(flow_x, first_lane, fresh_xx))

            curve_y = by_row(sub(rise_y, behind_y(rise_y)), valid)
            fresh_yy = settle(curve_y, yy_ref, t, THRESHOLD)
            flow_y = sub(ahead_y(fresh_yy), fresh_yy)
            total = add(total, sub(flow_y, behind_y(flow_y)))

            after = load(ref, t + 1)
            rise_t = sub(after, here)
            twice_t = times(rise_t, 2.0)
            fresh_xt = settle(sub(ahead_x(twice_t, last_lane), twice_t), xt_ref, t, 2.0 * THRESHOLD)
            bend = by_row(sub(ahead_y(rise_t), rise_t), twice_valid)
            fresh_yt = settle(bend, yt_ref, t, 2.0 * THRESHOLD)
            flow_t = add(sub(fresh_xt, behind_x(fresh_xt, first_lane)), sub(fresh_yt, behind_y(fresh_yt)))
            next_tt = settle(sub(sub(load(ref, t + 2), after), rise_t), tt_ref, t + 1, THRESHOLD)
            flow_t = add(flow_t, sub(next_tt, load(curve_ref, 0)))
            total = add(total, sub(flow_t, load(past_ref, 0)))
            store(past_ref, 0, flow_t)
            store(curve_ref, 0, next_tt)
            finish(t, here, total)

        def pair(k, carried):
            if before_pair is not None:
                before_pair(jnp.maximum(k - 1, 0))
            frame(2 * k)
            frame(2 * k + 1)
            if after_pair is not None:
                after_pair(k)
            return carried

        start = load(ref, 0)
        first_tt = settle(sub(sub(load(ref, 1), start), start), tt_ref, 0, THRESHOLD)
        store(curve_ref, 0, first_tt)
        store(past_ref, 0, first_tt)
        lax.fori_loop(0, count // 2, pair, 0)

    def finish_first(t, here, total):
        store(first_ref, t, sub(here, by_row(total, twice_step)))

    def finish_last(t, here, total):
        change = sub(load(guide_ref, t), here)
        update = sub(add(here, times(change, STEP_SIZE + 0.5)), times(total, 2.0 * STEP_SIZE))
        slot = lax.rem(t, 2) * block_rows
        for c in range(columns):
            for j in range(major):
                lines_ref[c, pl.ds(j, SUBLANES, stride=major), :] = update[j][c]
            high, low = high_low(lines_ref[c, pl.ds(REACH, block_rows), :])
            turned_ref[pl.ds(slot, block_rows), pl.ds(c * LANES, LANES)] = high
            turned_ref[pl.ds(2 * block_rows + slot, block_rows), pl.ds(c * LANES, LANES)] = low

    def reorder(k):
        both = dot(turned_ref[...], order_ref[...])
        both = both[:2 * block_rows] + both[2 * block_rows:]
        done_ref[pl.ds(2 * k, 2)] = both.reshape(2, block_rows, fine)

    def sending(k):
        return pltpu.make_async_copy(done_ref.at[pl.ds(2 * k, 2)], out_ref.at[pl.ds(2 * k, 2)], sent.at[k])

    def send_last(k):
        @pl.when(k > 0)
        def _():
            sending(k - 1).start()

    sweep(guide_ref, finish_first, False)
    close(first_ref)
    turned_ref[...] = jnp.zeros_like(turned_ref)
    sweep(first_ref, finish_last, True, reorder, send_last)
    reorder(count // 2 - 1)
    sending(count // 2 - 1).start()
    for k in range(count // 2):
        sending(k).wait()


def shards(raw_frames, angle_index, phase_index, band_shift):
    raw_count, coarse, _ = raw_frames.shape
    fine = 2 * coarse
    tm_count = lax.axis_size("tm")
    chips = tm_count // 2
    block_rows = fine // tm_count
    window_rows = block_rows + 2 * REACH
    chip_rows = 2 * block_rows + 2 * REACH
    wiener = wiener_table(fine)
    half_step = half_table(coarse)
    col_filter = wiener[columns_of(fine)][:, split_order(fine)]
    row_windows = row_filter(wiener, chips, 2 * block_rows)
    order = np.eye(fine, dtype=jnp.bfloat16)[columns_of(fine)]
    sources = (angle_index, phase_index, band_shift.T, raw_frames, half_step, col_filter, row_windows)
    vector = pl.BlockSpec(memory_space=pltpu.VMEM)
    frames = pl.pallas_call(
        filter_kernel,
        out_shape=[jax.ShapeDtypeStruct((chip_rows, fine), jnp.bfloat16)] * chips,
        in_specs=[pl.BlockSpec(memory_space=pltpu.HBM)] * len(sources),
        out_specs=[vector] * chips,
        scratch_shapes=[
            *[pltpu.SMEM(v.shape, v.dtype) for v in sources[:3]],
            *[pltpu.VMEM(v.shape, v.dtype) for v in sources[3:]],
            pltpu.VMEM((raw_count, fine, coarse), jnp.bfloat16), pltpu.VMEM((fine, fine), jnp.bfloat16),
            pltpu.VMEM((chips, chip_rows, fine), jnp.bfloat16), pltpu.SemaphoreType.DMA((len(sources),)),
        ],
        name="filter_group",
    )(*sources)
    offsets = [0] + exchange_order(chips)
    received = [frames[0]]
    for k in offsets[1:]:
        received.append(lax.ppermute(frames[k], "tm", [(i, i ^ (2 * k)) for i in range(tm_count)]))
    half = chips // 2
    partner = [
        pl.pallas_call(
            partner_kernel,
            out_shape=jax.ShapeDtypeStruct((half, window_rows, fine), jnp.bfloat16),
            in_specs=[vector] * half,
            out_specs=vector,
            compiler_params=pltpu.CompilerParams(vmem_limit_bytes=8 << 20),
            name="partner_rows",
        )(*part)
        for part in (received[:half], received[half:])
    ]
    partner = [lax.ppermute(v, "tm", [(i, i ^ 1) for i in range(tm_count)]) for v in partner]

    def field(frames):
        return pltpu.VMEM((frames, window_rows, fine), jnp.float32)

    return pl.pallas_call(
        partial(denoise_kernel, offsets=offsets),
        out_shape=jax.ShapeDtypeStruct((tm_count, block_rows, fine), jnp.float32),
        in_specs=[vector] * (chips + 3),
        out_specs=pl.BlockSpec(memory_space=pltpu.HBM),
        scratch_shapes=[
            pltpu.VMEM((tm_count, window_rows, fine), jnp.bfloat16),
            field(tm_count + 2), field(tm_count + 2), *[field(tm_count)] * 5, field(tm_count + 1),
            field(1), field(1), pltpu.VMEM((fine // LANES, window_rows, LANES), jnp.float32),
            pltpu.VMEM((4 * block_rows, fine), jnp.bfloat16),
            pltpu.VMEM((tm_count, block_rows, fine), jnp.float32), pltpu.SemaphoreType.DMA((chips,)),
        ],
        compiler_params=pltpu.CompilerParams(vmem_limit_bytes=40 << 20),
        name="denoise_rows",
    )(*received, *partner, order)


def solution(mesh):
    return jax.shard_map(
        shards,
        mesh=mesh,
        in_specs=(P(("grp", "tm"), None, None), P("grp"), P("grp"), P("grp", None)),
        out_specs=P("grp", "tm", None),
        check_vma=False,
    )
```
